128 devices in a mesh: occ: 16 (over x_lo, z, core), aux: 8 (over y, x_hi).
Axes of the slice: x: 4 (x_hi: 2, x_lo: 2; x = x_hi * 2 + x_lo), y: 4, z: 4, core: 2. Of those that a mesh axis runs over, the one named last changes fastest.
Arguments:
- integrals: bfloat16 [2048, 256, 512], P('aux', 'occ'), may hold values from -1.1953125 to 1.1953125
- metric: bfloat16 [2048, 2048], replicated, may hold values from -0.125 to 0.125
- e_occ: float32 [256], replicated, may hold values from -2 to -0.3
- e_vir: float32 [512], replicated, may hold values from 0.2 to 3
- partner: int32 [256, 2], P(('occ', 'aux')), may hold values from 0 to 1
- screen: int32 [256, 2], P(('occ', 'aux')), may hold values from 0 to 1
Outputs:
- gradient: bfloat16 [2048, 256, 512], P(None, ('occ', 'aux'))
- density: float32 [512, 512], P('occ')
The draws below stay inside these ranges and needn't reach their ends.
All inputs are finite; a program needn't handle non-finite values.
Results may differ from the reference program's by a relative error of at most 0.0055.
Values may be sent and summed in bfloat16 or wider, within the bound.
No kernel may reach another device: no remote copies, remote signals or barrier semaphores. Data moves between devices by JAX's collectives and lax.ppermute only.
A program may use at most 128 MiB of HBM per device.

```python
import jax
import jax.numpy as jnp
from jax import lax

NOCC = 256
NVIR = 512
NAUX = 2048
ROUNDS = 2
OWN = 2
N_OCC = 16
N_AUX = 8


def draw_screen(key, part):
    first, second = jax.random.split(jax.random.fold_in(key, 17))
    level = jax.random.randint(first, (NOCC // OWN, 1, 1), 1, 5)
    roll = jax.random.randint(second, (NOCC // OWN, OWN, ROUNDS), 0, 4)
    return (roll < level).astype(jnp.int32).reshape(NOCC, ROUNDS)


def touch_ends(entries, rng, low, top_value):
    extent = entries.shape
    place = [jax.random.randint(jax.random.fold_in(rng, axis), (), 0, extent[axis]) for axis in range(len(extent))]
    entries = entries.at[tuple(place)].set(low)
    longest = extent.index(max(extent))
    place[longest] = (place[longest] + 1) % extent[longest]
    return entries.at[tuple(place)].set(top_value)


def level_of(own_key, extent, cuts, smallest, largest):
    def one(dim, parts):
        heights = jax.random.uniform(jax.random.fold_in(jax.random.fold_in(own_key, 6), dim), (parts,), jnp.float32, smallest / len(cuts), largest / len(cuts))
        return jnp.repeat(jnp.exp(heights), extent[dim] // parts).reshape((-1,) + (1,) * (len(extent) - dim - 1))

    gain = one(*cuts[0])
    for cut in cuts[1:]:
        gain = gain * one(*cut)
    return gain


def normal_values(key, extent, spread, most, pieces=(), kind=jnp.bfloat16):
    array = jax.random.normal(key, extent, jnp.float32) * spread
    if len(pieces) > 0:
        array = level_of(key, extent, pieces, -0.22, 0.18) * array
    return jnp.clip(array, min=-most, max=most).astype(kind)


def setup_inputs(seed: int = 0) -> dict:
    keys = jax.random.split(jax.random.key(seed), 7)
    integrals = normal_values(keys[0], (NAUX, NOCC, NVIR), 0.17, 1.1953125, ((0, 8), (1, 16)))
    metric = normal_values(keys[1], (NAUX, NAUX), NAUX ** -0.5, 0.125)
    e_occ = jnp.clip(jax.random.uniform(keys[2], (NOCC,), jnp.float32, -2.0, -0.3), -2.0, -0.3)
    e_vir = jnp.clip(jax.random.uniform(keys[3], (NVIR,), jnp.float32, 0.2, 3.0), 0.2, 3.0)
    partner = touch_ends(jax.random.randint(keys[4], (NOCC, ROUNDS), 0, OWN), jax.random.fold_in(keys[4], 1), 0, OWN - 1).astype(jnp.int32)
    screen = draw_screen(jax.random.fold_in(keys[6], 71), 0)
    return {"integrals": integrals, "metric": metric, "e_occ": e_occ, "e_vir": e_vir, "partner": partner, "screen": screen}


def reference(integrals, metric, e_occ, e_vir, partner, screen):
    groups = N_OCC * N_AUX
    own = NOCC // groups
    flat = integrals.reshape(NAUX, NOCC * NVIR)
    coeff = jnp.dot(metric, flat, preferred_element_type=jnp.float32).astype(jnp.bfloat16).reshape(NAUX, NOCC, NVIR)
    pair_sum = e_vir[:, None] + e_vir[None, :]
    shifts = (1, groups // 2)

    def visit(density, index):
        gamma_row = jnp.zeros((NAUX, NVIR), jnp.float32)
        for rnd in range(ROUNDS):
            source = (index // own - shifts[rnd % 2]) % groups
            other = (source * own + partner[index, rnd]).astype(jnp.int32)
            left = lax.dynamic_index_in_dim(coeff, index, 1, False)
            right = lax.dynamic_index_in_dim(coeff, other, 1, False)
            intersection = lax.dot_general(left, right, (((0,), (0,)), ((), ())), preferred_element_type=jnp.float32)
            gap = pair_sum - e_occ[index] - e_occ[other]
            amp = (screen[index, rnd].astype(jnp.float32) * intersection / gap).astype(jnp.bfloat16)
            gamma_row = gamma_row + lax.dot_general(right, amp, (((1,), (1,)), ((), ())), preferred_element_type=jnp.float32)
            density = density + lax.dot_general(amp, amp, (((1,), (1,)), ((), ())), preferred_element_type=jnp.float32)
        return density, gamma_row.astype(jnp.bfloat16)

    start = jnp.zeros((NVIR, NVIR), jnp.float32)
    density, rows = lax.scan(visit, start, jnp.arange(NOCC, dtype=jnp.int32))
    gradient = jnp.transpose(rows, (1, 0, 2))
    return gradient, density / NOCC
```

```python
import jax
import jax.numpy as jnp
from jax import lax
from jax.experimental import pallas as pl
from jax.experimental.pallas import tpu as pltpu
from jax.sharding import PartitionSpec as P

NOCC = 256
AXES = ("occ", "aux")
ROWS = 256
VMEM = 60 * 1024 * 1024


def along_y(by):
    return lambda l: (l & ~6) | (((((l >> 1) & 3) + by) % 4) << 1)


def same_hop(l):
    return l ^ 64


def other_hop(l):
    return l ^ 65


def onward_hop(l):
    to = l ^ 65
    return to if to & 1 else (to + 2) % 128


def before_hop(by):
    def to(l):
        y = (((l >> 1) & 3) + by) % 4
        there = (l & ~6) | (y << 1)
        return (there + 8) % 128 if y == 0 else there

    return to


def send(array, to, after=(), only=lambda l: True):
    if after:
        array = lax.optimization_barrier((array, *after))[0]
    return lax.ppermute(array, AXES, [(l, to(l)) for l in range(128) if only(l)])


def transform_kernel(count, ids, *refs):
    metric = jnp.concatenate([ref[...] for ref in refs[:count]], axis=1)
    out = refs[-1]
    for slot in range(2):
        right = jnp.concatenate([ref[slot] for ref in refs[count : 2 * count]], axis=0)
        mixed = jnp.dot(metric, right, preferred_element_type=jnp.float32)
        out[slot] = mixed.astype(out.dtype)


def transform(metric, ids, pieces, tile=512):
    count = len(pieces)
    naux = metric.shape[0]
    nvir = pieces[0][0].shape[-1]
    columns = [
        pl.BlockSpec((tile, ROWS), lambda m, ids, k=k: (m, ids[k])) for k in range(count)
    ]
    rows = [
        pl.BlockSpec((None, 2, ROWS, nvir), lambda m, ids, n=n: (n, 0, 0, 0)) for _, n in pieces
    ]
    flops = 2 * naux * count * ROWS * 2 * nvir
    return pl.pallas_call(
        lambda *refs: transform_kernel(count, *refs),
        out_shape=jax.ShapeDtypeStruct((2, naux, nvir), jnp.bfloat16),
        grid_spec=pltpu.PrefetchScalarGridSpec(
            num_scalar_prefetch=1,
            grid=(naux // tile,),
            in_specs=columns + rows,
            out_specs=pl.BlockSpec((2, tile, nvir), lambda m, ids: (0, m, 0)),
        ),
        compiler_params=pltpu.CompilerParams(vmem_limit_bytes=VMEM),
        cost_estimate=pl.CostEstimate(
            flops=flops, bytes_accessed=2 * naux * naux + 8 * naux * nvir, transcendentals=0
        ),
        name="transform",
    )(ids, *([metric] * count), *[array for array, _ in pieces])


def pair_kernel(ints, floats, left, before, far, row, column, amps, density, total):
    slot = pl.program_id(0)
    pair_sum = column[...] + row[...]

    @pl.when(slot == 0)
    def _():
        total[...] = jnp.zeros_like(total)

    for rnd, rights in enumerate((before, far)):
        local = ints[slot, rnd]
        right = rights[local]
        intersection = lax.dot_general(
            left[0], right, (((0,), (0,)), ((), ())), preferred_element_type=jnp.float32
        )
        gap = pair_sum - floats[0, slot] - floats[1 + rnd, local]
        kept = ints[slot, 2 + rnd].astype(jnp.float32)
        amp = (kept * intersection / gap).astype(jnp.bfloat16)
        amps[0, rnd] = amp
        total[...] += lax.dot_general(
            amp, amp, (((1,), (1,)), ((), ())), preferred_element_type=jnp.float32
        )

    @pl.when(slot == 1)
    def _():
        density[...] = total[...].astype(jnp.bfloat16)


def pairs(ints, floats, own, before, far, e_vir):
    _, naux, nvir = own.shape
    whole = pl.BlockSpec((2, naux, nvir), lambda s: (0, 0, 0))
    smem = pl.BlockSpec(memory_space=pltpu.SMEM)
    return pl.pallas_call(
        pair_kernel,
        out_shape=(
            jax.ShapeDtypeStruct((2, 2, nvir, nvir), jnp.bfloat16),
            jax.ShapeDtypeStruct((nvir, nvir), jnp.bfloat16),
        ),
        grid=(2,),
        in_specs=[
            smem,
            smem,
            pl.BlockSpec((1, naux, nvir), lambda s: (s, 0, 0)),
            whole,
            whole,
            pl.BlockSpec((1, nvir), lambda s: (0, 0)),
            pl.BlockSpec((nvir, 1), lambda s: (0, 0)),
        ],
        out_specs=(
            pl.BlockSpec((1, 2, nvir, nvir), lambda s: (s, 0, 0, 0)),
            pl.BlockSpec((nvir, nvir), lambda s: (0, 0)),
        ),
        scratch_shapes=[pltpu.VMEM((nvir, nvir), jnp.float32)],
        compiler_params=pltpu.CompilerParams(vmem_limit_bytes=VMEM),
        cost_estimate=pl.CostEstimate(
            flops=8 * naux * nvir * nvir + 8 * nvir**3,
            bytes_accessed=12 * naux * nvir,
            transcendentals=0,
        ),
        name="pairs",
    )(ints, floats, own, before, far, e_vir[None, :], e_vir[:, None])


def gradient_kernel(ints, amps, before, far, out):
    for slot in range(2):
        total = None
        for rnd, rights in enumerate((before, far)):
            term = lax.dot_general(
                rights[ints[slot, rnd]],
                amps[slot, rnd],
                (((1,), (1,)), ((), ())),
                preferred_element_type=jnp.float32,
            )
            total = term if total is None else total + term
        out[:, slot, :] = total.astype(jnp.bfloat16)


def gradient_of(ints, amps, before, far, tile=256):
    _, naux, nvir = before.shape
    rows = pl.BlockSpec((2, tile, nvir), lambda m: (0, m, 0))
    return pl.pallas_call(
        gradient_kernel,
        out_shape=jax.ShapeDtypeStruct((naux, 2, nvir), jnp.bfloat16),
        grid=(naux // tile,),
        in_specs=[
            pl.BlockSpec(memory_space=pltpu.SMEM),
            pl.BlockSpec((2, 2, nvir, nvir), lambda m: (0, 0, 0, 0)),
            rows,
            rows,
        ],
        out_specs=pl.BlockSpec((tile, 2, nvir), lambda m: (m, 0, 0)),
        compiler_params=pltpu.CompilerParams(vmem_limit_bytes=VMEM),
        cost_estimate=pl.CostEstimate(
            flops=8 * naux * nvir * nvir, bytes_accessed=12 * naux * nvir, transcendentals=0
        ),
        name="gradient",
    )(ints, amps, before, far)


def summed_at_owner(array):
    pieces = array.reshape(16, -1, array.shape[1])
    arrived = lax.all_to_all(pieces, "occ", split_axis=0, concat_axis=0, tiled=True)
    return arrived.astype(jnp.float32).sum(axis=0)


def summed_for_everyone(array):
    copies = jnp.broadcast_to(array[None], (8, *array.shape))
    arrived = lax.all_to_all(copies, "aux", 0, 0, tiled=True)
    return arrived.astype(jnp.float32).sum(axis=0)


def on_device(integrals, metric, e_occ, e_vir, partner, screen):
    nvir = integrals.shape[-1]
    device = lax.axis_index(AXES)
    aux = lax.axis_index("aux")
    y, x_hi = aux // 2, aux % 2

    by_owner = jnp.transpose(integrals, (1, 0, 2)).reshape(8, 2, ROWS, nvir)

    def block(index):
        return lax.dynamic_index_in_dim(by_owner, index, 0, True)

    def for_row(k):
        there = (y + k) % 4 * 2
        return block(there + x_hi), block(there + 1 - x_hi)

    same0, other0 = for_row(0)
    a0s = send(same0, same_hop)
    a0o = send(other0, other_hop)
    y1 = send(jnp.concatenate(for_row(1)), along_y(1))
    y3 = send(jnp.concatenate(for_row(3)), along_y(3))
    half = send(jnp.concatenate(for_row(2)), along_y(3), (y1, y3))
    same1 = jnp.concatenate([y1[:1], y3[:1]])
    other1 = jnp.concatenate([y1[1:], y3[1:]])
    a1s = send(same1, same_hop, (a0s,))
    a1o = send(other1, other_hop, (a0o,))
    even = lambda l: l & 1 == 0
    ahead = {
        k: send(block(((y + k) % 4 * 2 + 7) % 8), before_hop(k), (y1, y3), even)
        for k in (0, 1, 2, 3)
    }
    y2 = send(half, along_y(3), (a1s,))
    b1s = send(jnp.concatenate([a0o, a1o]), same_hop, (a1s,))
    b1o = send(jnp.concatenate([a0s, a1s]), onward_hop, (a1o,))
    a2s = send(y2[:1], same_hop, (b1s, b1o))
    a2o = send(y2[1:], other_hop, (b1s, b1o))
    b2s = send(a2o, same_hop)
    b2o = send(a2s, onward_hop)

    order = jnp.array([0, 1, 3, 2], jnp.int32)
    here = (y - order) % 4 * 2
    near_ids = here + x_hi
    cross_ids = here + 1 - x_hi
    late_ids = jnp.where(x_hi == 0, (here + 6) % 8 + 1, cross_ids)
    own_ids = jnp.concatenate([near_ids, cross_ids]).astype(jnp.int32)
    before_ids = jnp.concatenate([near_ids, late_ids]).astype(jnp.int32)

    far = transform(
        metric, own_ids, [(a0s, 0), (a1s, 0), (a1s, 1), (a2s, 0), (a0o, 0), (a1o, 0), (a1o, 1), (a2o, 0)]
    )
    own = transform(
        metric, own_ids, [(same0, 0), (y1, 0), (y3, 0), (y2, 0), (b1s, 0), (b1s, 1), (b1s, 2), (b2s, 0)]
    )
    near = jnp.where(
        x_hi == 0,
        jnp.concatenate([ahead[0], ahead[1], ahead[3], ahead[2]]),
        jnp.concatenate([other0, other1, y2[1:]]),
    )
    before = transform(
        metric,
        before_ids,
        [(near, 0), (near, 1), (near, 2), (near, 3), (b1o, 0), (b1o, 1), (b1o, 2), (b2o, 0)],
    )

    ints = jnp.concatenate([partner, screen], axis=1).astype(jnp.int32)
    owners = jnp.stack([device, (device - 1) % 128, (device - 64) % 128])
    floats = e_occ[owners[:, None] * 2 + jnp.arange(2)[None, :]]
    amps, density = pairs(ints, floats, own, before, far, e_vir)
    gradient = gradient_of(ints, amps, before, far)
    rows = summed_at_owner(density)
    total = summed_for_everyone(rows.astype(jnp.bfloat16))
    return gradient, total / NOCC


def solution(mesh):
    placed = (P("aux", "occ", None), P(), P(), P(), P(AXES, None), P(AXES, None))
    return jax.shard_map(
        on_device,
        mesh=mesh,
        in_specs=placed,
        out_specs=(P(None, AXES, None), P("occ", None)),
        check_vma=False,
    )
```

```python
import jax
import jax.numpy as jnp
from jax import lax
from jax.experimental import pallas as pl
from jax.experimental.pallas import tpu as pltpu
from jax.sharding import PartitionSpec as P

NOCC = 256
AXES = ("occ", "aux")
ROWS = 256
VMEM = 60 * 1024 * 1024


def along_y(by):
    return lambda l: (l & ~6) | (((((l >> 1) & 3) + by) % 4) << 1)


def same_hop(l):
    return l ^ 64


def other_hop(l):
    return l ^ 65


def onward_hop(l):
    to = l ^ 65
    return to if to & 1 else (to + 2) % 128


def before_hop(by):
    def to(l):
        y = (((l >> 1) & 3) + by) % 4
        there = (l & ~6) | (y << 1)
        return (there + 8) % 128 if y == 0 else there

    return to


def send(array, to, after=(), only=lambda l: True):
    if after:
        array = lax.optimization_barrier((array, *after))[0]
    return lax.ppermute(array, AXES, [(l, to(l)) for l in range(128) if only(l)])


def transform_kernel(count, ids, *refs):
    metric = jnp.concatenate([ref[...] for ref in refs[:count]], axis=1)
    out = refs[-1]
    for slot in range(2):
        right = jnp.concatenate([ref[slot] for ref in refs[count : 2 * count]], axis=0)
        mixed = jnp.dot(metric, right, preferred_element_type=jnp.float32)
        if len(refs) == 2 * count + 2:
            mixed = mixed + refs[2 * count][slot]
        out[slot] = mixed.astype(out.dtype)


def transform(metric, ids, pieces, sofar=None, dtype=jnp.bfloat16, tile=512):
    count = len(pieces)
    naux = metric.shape[0]
    nvir = pieces[0][0].shape[-1]
    columns = [
        pl.BlockSpec((tile, ROWS), lambda m, ids, k=k: (m, ids[k])) for _, _, k in pieces
    ]
    rows = [
        pl.BlockSpec((None, 2, ROWS, nvir), lambda m, ids, n=n: (n, 0, 0, 0))
        for _, n, _ in pieces
    ]
    sums = pl.BlockSpec((2, tile, nvir), lambda m, ids: (0, m, 0))
    flops = 4 * naux * count * ROWS * nvir
    moved = 2 * naux * count * ROWS + 4 * count * ROWS * nvir
    moved += 2 * naux * nvir * ((4 if sofar is not None else 0) + jnp.dtype(dtype).itemsize)
    return pl.pallas_call(
        lambda *refs: transform_kernel(count, *refs),
        out_shape=jax.ShapeDtypeStruct((2, naux, nvir), dtype),
        grid_spec=pltpu.PrefetchScalarGridSpec(
            num_scalar_prefetch=1,
            grid=(naux // tile,),
            in_specs=columns + rows + ([] if sofar is None else [sums]),
            out_specs=sums,
        ),
        compiler_params=pltpu.CompilerParams(vmem_limit_bytes=VMEM),
        cost_estimate=pl.CostEstimate(flops=flops, bytes_accessed=moved, transcendentals=0),
        name="transform",
    )(
        ids,
        *([metric] * count),
        *[array for array, _, _ in pieces],
        *([] if sofar is None else [sofar]),
    )


def pair_kernel(ints, floats, left, before, far, row, column, amps, density, total):
    slot = pl.program_id(0)
    pair_sum = column[...] + row[...]

    @pl.when(slot == 0)
    def _():
        total[...] = jnp.zeros_like(total)

    for rnd, rights in enumerate((before, far)):
        local = ints[slot, rnd]
        right = rights[local]
        intersection = lax.dot_general(
            left[0], right, (((0,), (0,)), ((), ())), preferred_element_type=jnp.float32
        )
        gap = pair_sum - floats[0, slot] - floats[1 + rnd, local]
        kept = ints[slot, 2 + rnd].astype(jnp.float32)
        amp = (kept * intersection / gap).astype(jnp.bfloat16)
        amps[0, rnd] = amp
        total[...] += lax.dot_general(
            amp, amp, (((1,), (1,)), ((), ())), preferred_element_type=jnp.float32
        )

    @pl.when(slot == 1)
    def _():
        density[...] = total[...].astype(jnp.bfloat16)


def pairs(ints, floats, own, before, far, e_vir):
    _, naux, nvir = own.shape
    whole = pl.BlockSpec((2, naux, nvir), lambda s: (0, 0, 0))
    smem = pl.BlockSpec(memory_space=pltpu.SMEM)
    return pl.pallas_call(
        pair_kernel,
        out_shape=(
            jax.ShapeDtypeStruct((2, 2, nvir, nvir), jnp.bfloat16),
            jax.ShapeDtypeStruct((nvir, nvir), jnp.bfloat16),
        ),
        grid=(2,),
        in_specs=[
            smem,
            smem,
            pl.BlockSpec((1, naux, nvir), lambda s: (s, 0, 0)),
            whole,
            whole,
            pl.BlockSpec((1, nvir), lambda s: (0, 0)),
            pl.BlockSpec((nvir, 1), lambda s: (0, 0)),
        ],
        out_specs=(
            pl.BlockSpec((1, 2, nvir, nvir), lambda s: (s, 0, 0, 0)),
            pl.BlockSpec((nvir, nvir), lambda s: (0, 0)),
        ),
        scratch_shapes=[pltpu.VMEM((nvir, nvir), jnp.float32)],
        compiler_params=pltpu.CompilerParams(vmem_limit_bytes=VMEM),
        cost_estimate=pl.CostEstimate(
            flops=8 * naux * nvir * nvir + 8 * nvir**3,
            bytes_accessed=12 * naux * nvir,
            transcendentals=0,
        ),
        name="pairs",
    )(ints, floats, own, before, far, e_vir[None, :], e_vir[:, None])


def gradient_kernel(ints, amps, before, far, out):
    for slot in range(2):
        total = None
        for rnd, rights in enumerate((before, far)):
            term = lax.dot_general(
                rights[ints[slot, rnd]],
                amps[slot, rnd],
                (((1,), (1,)), ((), ())),
                preferred_element_type=jnp.float32,
            )
            total = term if total is None else total + term
        out[:, slot, :] = total.astype(jnp.bfloat16)


def gradient_of(ints, amps, before, far, tile=256):
    _, naux, nvir = before.shape
    rows = pl.BlockSpec((2, tile, nvir), lambda m: (0, m, 0))
    return pl.pallas_call(
        gradient_kernel,
        out_shape=jax.ShapeDtypeStruct((naux, 2, nvir), jnp.bfloat16),
        grid=(naux // tile,),
        in_specs=[
            pl.BlockSpec(memory_space=pltpu.SMEM),
            pl.BlockSpec((2, 2, nvir, nvir), lambda m: (0, 0, 0, 0)),
            rows,
            rows,
        ],
        out_specs=pl.BlockSpec((tile, 2, nvir), lambda m: (m, 0, 0)),
        compiler_params=pltpu.CompilerParams(vmem_limit_bytes=VMEM),
        cost_estimate=pl.CostEstimate(
            flops=8 * naux * nvir * nvir, bytes_accessed=12 * naux * nvir, transcendentals=0
        ),
        name="gradient",
    )(ints, amps, before, far)


def summed_at_owner(array):
    pieces = array.reshape(16, -1, array.shape[1])
    arrived = lax.all_to_all(pieces, "occ", split_axis=0, concat_axis=0, tiled=True)
    return arrived.astype(jnp.float32).sum(axis=0)


def summed_for_everyone(array):
    copies = jnp.broadcast_to(array[None], (8, *array.shape))
    arrived = lax.all_to_all(copies, "aux", 0, 0, tiled=True)
    return arrived.astype(jnp.float32).sum(axis=0)


def on_device(integrals, metric, e_occ, e_vir, partner, screen):
    nvir = integrals.shape[-1]
    device = lax.axis_index(AXES)
    aux = lax.axis_index("aux")
    y, x_hi = aux // 2, aux % 2

    by_owner = jnp.transpose(integrals, (1, 0, 2)).reshape(8, 2, ROWS, nvir)

    def block(index):
        return lax.dynamic_index_in_dim(by_owner, index, 0, True)

    def for_row(k):
        there = (y + k) % 4 * 2
        return block(there + x_hi), block(there + 1 - x_hi)

    same0, other0 = for_row(0)
    a0s = send(same0, same_hop)
    a0o = send(other0, other_hop)
    y1 = send(jnp.concatenate(for_row(1)), along_y(1))
    y3 = send(jnp.concatenate(for_row(3)), along_y(3))
    third = jnp.concatenate(for_row(2))
    even = lambda l: l & 1 == 0
    block_ahead = {k: block(((y + k) % 4 * 2 + 7) % 8) for k in range(4)}
    y1, y3, a0s, a0o, third, block_ahead = lax.optimization_barrier(
        (y1, y3, a0s, a0o, third, block_ahead)
    )
    half = send(third, along_y(3))
    same1 = jnp.concatenate([y1[:1], y3[:1]])
    other1 = jnp.concatenate([y1[1:], y3[1:]])
    a1s = send(same1, same_hop)
    a1o = send(other1, other_hop)
    ahead = {k: send(block_ahead[k], before_hop(k), (), even) for k in range(4)}
    y2 = send(half, along_y(3), (a1s,))
    b1s = send(jnp.concatenate([a0o, a1o]), same_hop, (a1s, *ahead.values()))
    b1o = send(jnp.concatenate([a0s, a1s]), onward_hop, (a1o, *ahead.values()))
    a2s = send(y2[:1], same_hop, (b1s, b1o))
    a2o = send(y2[1:], other_hop, (b1s, b1o))
    b2s = send(a2o, same_hop)
    b2o = send(a2s, onward_hop)

    order = jnp.array([0, 1, 3, 2], jnp.int32)
    here = (y - order) % 4 * 2
    near_ids = here + x_hi
    cross_ids = here + 1 - x_hi
    late_ids = jnp.where(x_hi == 0, (here + 6) % 8 + 1, cross_ids)
    own_ids = jnp.concatenate([near_ids, cross_ids]).astype(jnp.int32)
    before_ids = jnp.concatenate([near_ids, late_ids]).astype(jnp.int32)

    wide = jnp.float32
    far = transform(
        metric,
        own_ids,
        [(a0s, 0, 0), (a1s, 0, 1), (a1s, 1, 2), (a0o, 0, 4), (a1o, 0, 5), (a1o, 1, 6)],
        dtype=wide,
    )
    own = transform(
        metric,
        own_ids,
        [(same0, 0, 0), (y1, 0, 1), (y3, 0, 2), (y2, 0, 3), (b1s, 0, 4), (b1s, 1, 5), (b1s, 2, 6)],
        dtype=wide,
    )
    near = jnp.where(
        x_hi == 0,
        jnp.concatenate([ahead[0], ahead[1], ahead[3], ahead[2]]),
        jnp.concatenate([other0, other1, y2[1:]]),
    )
    before = transform(
        metric,
        before_ids,
        [(near, k, k) for k in range(4)] + [(b1o, k, 4 + k) for k in range(3)],
        dtype=wide,
    )
    far = transform(metric, own_ids, [(a2s, 0, 3), (a2o, 0, 7)], far)
    own = transform(metric, own_ids, [(b2s, 0, 7)], own)
    before = transform(metric, before_ids, [(b2o, 0, 7)], before)

    ints = jnp.concatenate([partner, screen], axis=1).astype(jnp.int32)
    owners = jnp.stack([device, (device - 1) % 128, (device - 64) % 128])
    floats = e_occ[owners[:, None] * 2 + jnp.arange(2)[None, :]]
    amps, density = pairs(ints, floats, own, before, far, e_vir)
    gradient = gradient_of(ints, amps, before, far)
    rows = summed_at_owner(density)
    total = summed_for_everyone(rows.astype(jnp.bfloat16))
    return gradient, total / NOCC


def solution(mesh):
    placed = (P("aux", "occ", None), P(), P(), P(), P(AXES, None), P(AXES, None))
    return jax.shard_map(
        on_device,
        mesh=mesh,
        in_specs=placed,
        out_specs=(P(None, AXES, None), P("occ", None)),
        check_vma=False,
    )
```

```python
import jax
import jax.numpy as jnp
from jax import lax
from jax.experimental import pallas as pl
from jax.experimental.pallas import tpu as pltpu
from jax.sharding import PartitionSpec as P

NOCC = 256
AXES = ("occ", "aux")
ROWS = 256
VMEM = 60 * 1024 * 1024


def along_y(by):
    return lambda l: (l & ~6) | (((((l >> 1) & 3) + by) % 4) << 1)


def same_hop(l):
    return l ^ 64


def other_hop(l):
    return l ^ 65


def crossing(l):
    return l & 63 == 63


def onward_hop(l):
    if crossing(l):
        return (l + 1) % 128
    to = l ^ 65
    return to if to & 1 else (to + 2) % 128


def next_row(l):
    return l if l & 1 else (l + 2) % 128


def send(array, to, after=(), only=lambda l: True):
    if after:
        array = lax.optimization_barrier((array, *after))[0]
    return lax.ppermute(array, AXES, [(l, to(l)) for l in range(128) if only(l)])


def transform_kernel(count, ids, *refs):
    metric = jnp.concatenate([ref[...] for ref in refs[:count]], axis=1)
    out = refs[-1]
    for slot in range(2):
        right = jnp.concatenate([ref[slot] for ref in refs[count : 2 * count]], axis=0)
        mixed = jnp.dot(metric, right, preferred_element_type=jnp.float32)
        if len(refs) == 2 * count + 2:
            mixed = mixed + refs[2 * count][slot]
        out[slot] = mixed.astype(out.dtype)


def transform(metric, ids, pieces, sofar=None, dtype=jnp.bfloat16, tile=512):
    count = len(pieces)
    naux = metric.shape[0]
    nvir = pieces[0][0].shape[-1]
    columns = [
        pl.BlockSpec((tile, ROWS), lambda m, ids, k=k: (m, ids[k])) for _, _, k in pieces
    ]
    rows = [
        pl.BlockSpec((None, 2, ROWS, nvir), lambda m, ids, n=n: (n, 0, 0, 0))
        for _, n, _ in pieces
    ]
    sums = pl.BlockSpec((2, tile, nvir), lambda m, ids: (0, m, 0))
    flops = 4 * naux * count * ROWS * nvir
    moved = 2 * naux * count * ROWS + 4 * count * ROWS * nvir
    moved += 2 * naux * nvir * ((4 if sofar is not None else 0) + jnp.dtype(dtype).itemsize)
    return pl.pallas_call(
        lambda *refs: transform_kernel(count, *refs),
        out_shape=jax.ShapeDtypeStruct((2, naux, nvir), dtype),
        grid_spec=pltpu.PrefetchScalarGridSpec(
            num_scalar_prefetch=1,
            grid=(naux // tile,),
            in_specs=columns + rows + ([] if sofar is None else [sums]),
            out_specs=sums,
        ),
        compiler_params=pltpu.CompilerParams(vmem_limit_bytes=VMEM),
        cost_estimate=pl.CostEstimate(flops=flops, bytes_accessed=moved, transcendentals=0),
        name="transform",
    )(
        ids,
        *([metric] * count),
        *[array for array, _, _ in pieces],
        *([] if sofar is None else [sofar]),
    )


def pair_kernel(ints, floats, left, before, far, row, column, amps, density, total):
    slot = pl.program_id(0)
    pair_sum = column[...] + row[...]

    @pl.when(slot == 0)
    def _():
        total[...] = jnp.zeros_like(total)

    for rnd, rights in enumerate((before, far)):
        local = ints[slot, rnd]
        right = rights[local]
        intersection = lax.dot_general(
            left[0], right, (((0,), (0,)), ((), ())), preferred_element_type=jnp.float32
        )
        gap = pair_sum - floats[0, slot] - floats[1 + rnd, local]
        kept = ints[slot, 2 + rnd].astype(jnp.float32)
        amp = (kept * intersection / gap).astype(jnp.bfloat16)
        amps[0, rnd] = amp
        total[...] += lax.dot_general(
            amp, amp, (((1,), (1,)), ((), ())), preferred_element_type=jnp.float32
        )

    @pl.when(slot == 1)
    def _():
        density[...] = total[...].astype(jnp.bfloat16)


def pairs(ints, floats, own, before, far, e_vir):
    _, naux, nvir = own.shape
    whole = pl.BlockSpec((2, naux, nvir), lambda s: (0, 0, 0))
    smem = pl.BlockSpec(memory_space=pltpu.SMEM)
    return pl.pallas_call(
        pair_kernel,
        out_shape=(
            jax.ShapeDtypeStruct((2, 2, nvir, nvir), jnp.bfloat16),
            jax.ShapeDtypeStruct((nvir, nvir), jnp.bfloat16),
        ),
        grid=(2,),
        in_specs=[
            smem,
            smem,
            pl.BlockSpec((1, naux, nvir), lambda s: (s, 0, 0)),
            whole,
            whole,
            pl.BlockSpec((1, nvir), lambda s: (0, 0)),
            pl.BlockSpec((nvir, 1), lambda s: (0, 0)),
        ],
        out_specs=(
            pl.BlockSpec((1, 2, nvir, nvir), lambda s: (s, 0, 0, 0)),
            pl.BlockSpec((nvir, nvir), lambda s: (0, 0)),
        ),
        scratch_shapes=[pltpu.VMEM((nvir, nvir), jnp.float32)],
        compiler_params=pltpu.CompilerParams(vmem_limit_bytes=VMEM),
        cost_estimate=pl.CostEstimate(
            flops=8 * naux * nvir * nvir + 8 * nvir**3,
            bytes_accessed=12 * naux * nvir,
            transcendentals=0,
        ),
        name="pairs",
    )(ints, floats, own, before, far, e_vir[None, :], e_vir[:, None])


def gradient_kernel(ints, amps, before, far, out):
    for slot in range(2):
        total = None
        for rnd, rights in enumerate((before, far)):
            term = lax.dot_general(
                rights[ints[slot, rnd]],
                amps[slot, rnd],
                (((1,), (1,)), ((), ())),
                preferred_element_type=jnp.float32,
            )
            total = term if total is None else total + term
        out[:, slot, :] = total.astype(jnp.bfloat16)


def gradient_of(ints, amps, before, far, tile=256):
    _, naux, nvir = before.shape
    rows = pl.BlockSpec((2, tile, nvir), lambda m: (0, m, 0))
    return pl.pallas_call(
        gradient_kernel,
        out_shape=jax.ShapeDtypeStruct((naux, 2, nvir), jnp.bfloat16),
        grid=(naux // tile,),
        in_specs=[
            pl.BlockSpec(memory_space=pltpu.SMEM),
            pl.BlockSpec((2, 2, nvir, nvir), lambda m: (0, 0, 0, 0)),
            rows,
            rows,
        ],
        out_specs=pl.BlockSpec((tile, 2, nvir), lambda m: (m, 0, 0)),
        compiler_params=pltpu.CompilerParams(vmem_limit_bytes=VMEM),
        cost_estimate=pl.CostEstimate(
            flops=8 * naux * nvir * nvir, bytes_accessed=12 * naux * nvir, transcendentals=0
        ),
        name="gradient",
    )(ints, amps, before, far)


def summed_at_owner(array):
    pieces = array.reshape(16, -1, array.shape[1])
    arrived = lax.all_to_all(pieces, "occ", split_axis=0, concat_axis=0, tiled=True)
    return arrived.astype(jnp.float32).sum(axis=0)


def summed_for_everyone(array):
    copies = jnp.broadcast_to(array[None], (8, *array.shape))
    arrived = lax.all_to_all(copies, "aux", 0, 0, tiled=True)
    return arrived.astype(jnp.float32).sum(axis=0)


def on_device(integrals, metric, e_occ, e_vir, partner, screen):
    nvir = integrals.shape[-1]
    device = lax.axis_index(AXES)
    aux = lax.axis_index("aux")
    y, x_hi = aux // 2, aux % 2

    by_owner = jnp.transpose(integrals, (1, 0, 2)).reshape(8, 2, ROWS, nvir)

    def block(index):
        return lax.dynamic_index_in_dim(by_owner, index, 0, True)

    def for_row(k):
        there = (y + k) % 4 * 2
        return block(there + x_hi), block(there + 1 - x_hi)

    order = jnp.array([0, 1, 3, 2], jnp.int32)
    here = (y - order) % 4 * 2
    own_ids = jnp.concatenate([here + x_hi, here + 1 - x_hi]).astype(jnp.int32)
    shifted = (here + 6 * (1 - x_hi)) % 8
    before_ids = jnp.concatenate([shifted + x_hi, shifted + 1 - x_hi]).astype(jnp.int32)

    wide = jnp.float32
    same0, other0 = for_row(0)
    a0s = send(same0, same_hop)
    a0o = send(other0, other_hop)
    y1 = send(jnp.concatenate(for_row(1)), along_y(1))
    y3 = send(jnp.concatenate(for_row(3)), along_y(3))
    y1, y3, a0s, a0o, third = lax.optimization_barrier(
        (y1, y3, a0s, a0o, jnp.concatenate(for_row(2)))
    )
    crosses = (device & 63) == 63

    def onward(mine, passing):
        return send(jnp.where(crosses, mine, passing), onward_hop)

    same1 = jnp.concatenate([y1[:1], y3[:1]])
    other1 = jnp.concatenate([y1[1:], y3[1:]])
    a1s = send(same1, same_hop)
    a1o = send(other1, other_hop)
    half = send(third, along_y(3))
    b0s = send(a0o, same_hop)
    b0o = onward(same0, a0s)
    r1 = send(jnp.concatenate([other0, other1]), next_row)
    a1s, a1o, half, b0s, b0o = lax.optimization_barrier((a1s, a1o, half, b0s, b0o))
    y2 = send(half, along_y(3))
    b1s = send(a1o, same_hop)
    b1o = onward(same1, a1s)
    far = transform(
        metric,
        own_ids,
        [(a0s, 0, 0), (a1s, 0, 1), (a1s, 1, 2), (a0o, 0, 4), (a1o, 0, 5), (a1o, 1, 6)],
        dtype=wide,
    )
    y2, b1s, b1o, r1, far = lax.optimization_barrier((y2, b1s, b1o, r1, far))
    a2s = send(y2[:1], same_hop)
    a2o = send(y2[1:], other_hop)
    own = transform(
        metric,
        own_ids,
        [(same0, 0, 0), (y1, 0, 1), (y3, 0, 2), (y2, 0, 3), (b0s, 0, 4), (b1s, 0, 5), (b1s, 1, 6)],
        dtype=wide,
    )
    a2s, a2o, own = lax.optimization_barrier((a2s, a2o, own))
    r2 = send(y2[1:], next_row)
    b2s = send(a2o, same_hop)
    b2o = onward(y2[:1], a2s)

    before = transform(
        metric,
        before_ids,
        [(r1, 0, 0), (r1, 1, 1), (r1, 2, 2), (b0o, 0, 4), (b1o, 0, 5), (b1o, 1, 6)],
        dtype=wide,
    )
    far = transform(metric, own_ids, [(a2s, 0, 3), (a2o, 0, 7)], far)
    own = transform(metric, own_ids, [(b2s, 0, 7)], own)
    before = transform(metric, before_ids, [(r2, 0, 3), (b2o, 0, 7)], before)

    ints = jnp.concatenate([partner, screen], axis=1).astype(jnp.int32)
    owners = jnp.stack([device, (device - 1) % 128, (device - 64) % 128])
    floats = e_occ[owners[:, None] * 2 + jnp.arange(2)[None, :]]
    amps, density = pairs(ints, floats, own, before, far, e_vir)
    gradient = gradient_of(ints, amps, before, far)
    rows = summed_at_owner(density)
    total = summed_for_everyone(rows.astype(jnp.bfloat16))
    return gradient, total / NOCC


def solution(mesh):
    placed = (P("aux", "occ", None), P(), P(), P(), P(AXES, None), P(AXES, None))
    return jax.shard_map(
        on_device,
        mesh=mesh,
        in_specs=placed,
        out_specs=(P(None, AXES, None), P("occ", None)),
        check_vma=False,
    )
```

```python
import jax
import jax.numpy as jnp
from jax import lax
from jax.experimental import pallas as pl
from jax.experimental.pallas import tpu as pltpu
from jax.sharding import PartitionSpec as P

NOCC = 256
AXES = ("occ", "aux")
ROWS = 256
VMEM = 60 * 1024 * 1024


def along_y(by):
    return lambda l: (l & ~6) | (((((l >> 1) & 3) + by) % 4) << 1)


def same_hop(l):
    return l ^ 64


def other_hop(l):
    return l ^ 65


def crossing(l):
    return l & 63 == 63


def onward_hop(l):
    if crossing(l):
        return (l + 1) % 128
    to = l ^ 65
    return to if to & 1 else (to + 2) % 128


def next_row(l):
    return l if l & 1 else (l + 2) % 128


def to_row(by):
    def to(l):
        if l & 1:
            return l
        y = (((l >> 1) & 3) + by) % 4
        there = (l & ~6) | (y << 1)
        return (there + 8) % 128 if y == 0 else there

    return to


def send(array, to, after=(), only=lambda l: True):
    if after:
        array = lax.optimization_barrier((array, *after))[0]
    return lax.ppermute(array, AXES, [(l, to(l)) for l in range(128) if only(l)])


def transform_kernel(count, ids, *refs):
    metric = jnp.concatenate([ref[...] for ref in refs[:count]], axis=1)
    out = refs[-1]
    for slot in range(2):
        right = jnp.concatenate([ref[slot] for ref in refs[count : 2 * count]], axis=0)
        mixed = jnp.dot(metric, right, preferred_element_type=jnp.float32)
        if len(refs) == 2 * count + 2:
            mixed = mixed + refs[2 * count][slot]
        out[slot] = mixed.astype(out.dtype)


def transform(metric, ids, pieces, sofar=None, dtype=jnp.bfloat16, tile=512):
    count = len(pieces)
    naux = metric.shape[0]
    nvir = pieces[0][0].shape[-1]
    columns = [
        pl.BlockSpec((tile, ROWS), lambda m, ids, k=k: (m, ids[k])) for _, _, k in pieces
    ]
    rows = [
        pl.BlockSpec((None, 2, ROWS, nvir), lambda m, ids, n=n: (n, 0, 0, 0))
        for _, n, _ in pieces
    ]
    sums = pl.BlockSpec((2, tile, nvir), lambda m, ids: (0, m, 0))
    flops = 4 * naux * count * ROWS * nvir
    moved = 2 * naux * count * ROWS + 4 * count * ROWS * nvir
    moved += 2 * naux * nvir * ((4 if sofar is not None else 0) + jnp.dtype(dtype).itemsize)
    return pl.pallas_call(
        lambda *refs: transform_kernel(count, *refs),
        out_shape=jax.ShapeDtypeStruct((2, naux, nvir), dtype),
        grid_spec=pltpu.PrefetchScalarGridSpec(
            num_scalar_prefetch=1,
            grid=(naux // tile,),
            in_specs=columns + rows + ([] if sofar is None else [sums]),
            out_specs=sums,
        ),
        compiler_params=pltpu.CompilerParams(vmem_limit_bytes=VMEM),
        cost_estimate=pl.CostEstimate(flops=flops, bytes_accessed=moved, transcendentals=0),
        name="transform",
    )(
        ids,
        *([metric] * count),
        *[array for array, _, _ in pieces],
        *([] if sofar is None else [sofar]),
    )


def finish_kernel(
    ids,
    ints,
    floats,
    m_far,
    m_cross,
    m_late,
    own_sum,
    before_sum,
    far_sum,
    b2s,
    b2o,
    a2s,
    a2o,
    row,
    column,
    amps,
    density,
    before,
    far,
    meet,
):
    step = pl.program_id(0)

    @pl.when(step == 0)
    def _():
        meet[...] = jnp.zeros_like(meet)

    def closed(sofar, slot, *terms):
        for metric, piece in terms:
            sofar = sofar + jnp.dot(
                metric[...], piece[0, slot], preferred_element_type=jnp.float32
            )
        return sofar.astype(jnp.bfloat16)

    for slot in range(2):
        before[slot] = closed(before_sum[slot], slot, (m_late, b2o))
        far[slot] = closed(far_sum[slot], slot, (m_far, a2s), (m_cross, a2o))
    for slot in range(2):
        left = closed(own_sum[slot], slot, (m_cross, b2s)).T
        for rnd, rights in enumerate((before, far)):
            right = rights[ints[slot, rnd]]
            meet[slot, rnd] += jnp.dot(left, right, preferred_element_type=jnp.float32)

    @pl.when(step == pl.num_programs(0) - 1)
    def _():
        pair_sum = column[...] + row[...]
        total = jnp.zeros(density.shape, jnp.float32)
        for slot in range(2):
            for rnd in range(2):
                gap = pair_sum - floats[0, slot] - floats[1 + rnd, ints[slot, rnd]]
                kept = ints[slot, 2 + rnd].astype(jnp.float32)
                amp = (kept * meet[slot, rnd] / gap).astype(jnp.bfloat16)
                amps[slot, rnd] = amp
                total = total + lax.dot_general(
                    amp, amp, (((1,), (1,)), ((), ())), preferred_element_type=jnp.float32
                )
        density[...] = total.astype(jnp.bfloat16)


def finish(ids, ints, floats, metric, own, before, far, b2s, b2o, a2s, a2o, e_vir, tile=512):
    _, naux, nvir = own.shape
    smem = pl.BlockSpec(memory_space=pltpu.SMEM)
    sums = pl.BlockSpec((2, tile, nvir), lambda m, ids: (0, m, 0))
    piece = pl.BlockSpec((1, 2, ROWS, nvir), lambda m, ids: (0, 0, 0, 0))
    columns = [pl.BlockSpec((tile, ROWS), lambda m, ids, k=k: (m, ids[k])) for k in range(3)]
    full = jax.ShapeDtypeStruct((2, naux, nvir), jnp.bfloat16)
    return pl.pallas_call(
        finish_kernel,
        out_shape=(
            jax.ShapeDtypeStruct((2, 2, nvir, nvir), jnp.bfloat16),
            jax.ShapeDtypeStruct((nvir, nvir), jnp.bfloat16),
            full,
            full,
        ),
        grid_spec=pltpu.PrefetchScalarGridSpec(
            num_scalar_prefetch=1,
            grid=(naux // tile,),
            in_specs=[smem, smem, *columns, sums, sums, sums, piece, piece, piece, piece]
            + [
                pl.BlockSpec((1, nvir), lambda m, ids: (0, 0)),
                pl.BlockSpec((nvir, 1), lambda m, ids: (0, 0)),
            ],
            out_specs=(
                pl.BlockSpec((2, 2, nvir, nvir), lambda m, ids: (0, 0, 0, 0)),
                pl.BlockSpec((nvir, nvir), lambda m, ids: (0, 0)),
                sums,
                sums,
            ),
            scratch_shapes=[pltpu.VMEM((2, 2, nvir, nvir), jnp.float32)],
        ),
        compiler_params=pltpu.CompilerParams(vmem_limit_bytes=VMEM),
        cost_estimate=pl.CostEstimate(
            flops=16 * naux * ROWS * nvir + 8 * naux * nvir * nvir + 8 * nvir**3,
            bytes_accessed=32 * naux * nvir,
            transcendentals=0,
        ),
        name="finish",
    )(
        ids,
        ints,
        floats,
        metric,
        metric,
        metric,
        own,
        before,
        far,
        b2s,
        b2o,
        a2s,
        a2o,
        e_vir[None, :],
        e_vir[:, None],
    )


def gradient_kernel(ints, amps, before, far, *rest):
    out = rest[-1]
    for slot in range(2):
        total = None
        for rnd, rights in enumerate((before, far)):
            term = lax.dot_general(
                rights[ints[slot, rnd]],
                amps[slot, rnd],
                (((1,), (1,)), ((), ())),
                preferred_element_type=jnp.float32,
            )
            total = term if total is None else total + term
        out[:, slot, :] = total.astype(jnp.bfloat16)


def gradient_of(ints, amps, before, far, upper=None, tile=256):
    _, naux, nvir = before.shape
    steps = naux // tile // 2
    first = 0 if upper is None else steps
    rows = pl.BlockSpec((2, tile, nvir), lambda m: (0, m + first, 0))
    rest = () if upper is None else (upper,)
    return pl.pallas_call(
        gradient_kernel,
        out_shape=jax.ShapeDtypeStruct((naux, 2, nvir), jnp.bfloat16),
        grid=(steps,),
        in_specs=[
            pl.BlockSpec(memory_space=pltpu.SMEM),
            pl.BlockSpec((2, 2, nvir, nvir), lambda m: (0, 0, 0, 0)),
            rows,
            rows,
        ]
        + [pl.BlockSpec(memory_space=pl.ANY)] * len(rest),
        out_specs=pl.BlockSpec((tile, 2, nvir), lambda m: (m + first, 0, 0)),
        input_output_aliases={4: 0} if rest else {},
        compiler_params=pltpu.CompilerParams(vmem_limit_bytes=VMEM),
        cost_estimate=pl.CostEstimate(
            flops=4 * naux * nvir * nvir, bytes_accessed=6 * naux * nvir, transcendentals=0
        ),
        name="gradient",
    )(ints, amps, before, far, *rest)


def summed_at_owner(array):
    pieces = array.reshape(16, -1, array.shape[1])
    arrived = lax.all_to_all(pieces, "occ", split_axis=0, concat_axis=0, tiled=True)
    return arrived.astype(jnp.float32).sum(axis=0)


def summed_for_everyone(array):
    copies = jnp.broadcast_to(array[None], (8, *array.shape))
    arrived = lax.all_to_all(copies, "aux", 0, 0, tiled=True)
    return arrived.astype(jnp.float32).sum(axis=0)


def on_device(integrals, metric, e_occ, e_vir, partner, screen):
    nvir = integrals.shape[-1]
    device = lax.axis_index(AXES)
    aux = lax.axis_index("aux")
    y, x_hi = aux // 2, aux % 2

    by_owner = jnp.transpose(integrals, (1, 0, 2)).reshape(8, 2, ROWS, nvir)

    def block(index):
        return lax.dynamic_index_in_dim(by_owner, index, 0, True)

    def for_row(k):
        there = (y + k) % 4 * 2
        return block(there + x_hi), block(there + 1 - x_hi)

    order = jnp.array([0, 1, 3, 2], jnp.int32)
    here = (y - order) % 4 * 2
    own_ids = jnp.concatenate([here + x_hi, here + 1 - x_hi]).astype(jnp.int32)
    shifted = (here + 6 * (1 - x_hi)) % 8
    before_ids = jnp.concatenate([shifted + x_hi, shifted + 1 - x_hi]).astype(jnp.int32)

    wide = jnp.float32
    same0, other0 = for_row(0)
    a0s = send(same0, same_hop)
    a0o = send(other0, other_hop)
    y1 = send(jnp.concatenate(for_row(1)), along_y(1))
    y3 = send(jnp.concatenate(for_row(3)), along_y(3))
    y1, y3, a0s, a0o, third, here0, below0 = lax.optimization_barrier(
        (
            y1,
            y3,
            a0s,
            a0o,
            jnp.concatenate(for_row(2)),
            block((y * 2 + 7) % 8),
            block((y * 2 + 5) % 8),
        )
    )
    crosses = (device & 63) == 63

    def onward(mine, passing):
        return send(jnp.where(crosses, mine, passing), onward_hop)

    same1 = jnp.concatenate([y1[:1], y3[:1]])
    other1 = jnp.concatenate([y1[1:], y3[1:]])
    a1s = send(same1, same_hop)
    a1o = send(other1, other_hop)
    half = send(third, along_y(3))
    b0s = send(a0o, same_hop)
    b0o = onward(same0, a0s)
    r1 = send(jnp.concatenate([other0, y1[1:]]), next_row)
    near0 = send(jnp.where(x_hi == 0, here0, y3[1:]), to_row(0))
    near3 = send(below0, to_row(3), (), lambda l: l & 1 == 0)
    a1s, a1o, half, b0s, b0o = lax.optimization_barrier((a1s, a1o, half, b0s, b0o))
    y2 = send(half, along_y(3))
    b1s = send(a1o, same_hop)
    b1o = onward(same1, a1s)
    far = transform(
        metric,
        own_ids,
        [(a0s, 0, 0), (a1s, 0, 1), (a1s, 1, 2), (a0o, 0, 4), (a1o, 0, 5), (a1o, 1, 6)],
        dtype=wide,
    )
    y2, b1s, b1o, r1, near0, near3, far = lax.optimization_barrier(
        (y2, b1s, b1o, r1, near0, near3, far)
    )
    a2s = send(y2[:1], same_hop)
    a2o = send(y2[1:], other_hop)
    own = transform(
        metric,
        own_ids,
        [(same0, 0, 0), (y1, 0, 1), (y3, 0, 2), (y2, 0, 3), (b0s, 0, 4), (b1s, 0, 5), (b1s, 1, 6)],
        dtype=wide,
    )
    a2s, a2o, own = lax.optimization_barrier((a2s, a2o, own))
    near2 = jnp.where(x_hi == 0, near3, y2[1:])
    b2s = send(a2o, same_hop)
    b2o = onward(y2[:1], a2s)

    before = transform(
        metric,
        before_ids,
        [
            (r1, 0, 0),
            (r1, 1, 1),
            (near0, 0, 2),
            (near2, 0, 3),
            (b0o, 0, 4),
            (b1o, 0, 5),
            (b1o, 1, 6),
        ],
        dtype=wide,
    )

    ints = jnp.concatenate([partner, screen], axis=1).astype(jnp.int32)
    owners = jnp.stack([device, (device - 1) % 128, (device - 64) % 128])
    floats = e_occ[owners[:, None] * 2 + jnp.arange(2)[None, :]]
    ids = jnp.stack([own_ids[3], own_ids[7], before_ids[7]])
    amps, density, before, far = finish(
        ids, ints, floats, metric, own, before, far, b2s, b2o, a2s, a2o, e_vir
    )
    gradient = gradient_of(ints, amps, before, far)
    rows = summed_at_owner(density).astype(jnp.bfloat16)
    rows, amps = lax.optimization_barrier((rows, amps))
    gradient = gradient_of(ints, amps, before, far, gradient)
    return gradient, summed_for_everyone(rows) / NOCC


def solution(mesh):
    placed = (P("aux", "occ", None), P(), P(), P(), P(AXES, None), P(AXES, None))
    return jax.shard_map(
        on_device,
        mesh=mesh,
        in_specs=placed,
        out_specs=(P(None, AXES, None), P("occ", None)),
        check_vma=False,
    )
```

```python
import jax
import jax.numpy as jnp
from jax import lax
from jax.experimental import pallas as pl
from jax.experimental.pallas import tpu as pltpu
from jax.sharding import PartitionSpec as P

NOCC = 256
AXES = ("occ", "aux")
ROWS = 256


def along_y(by):
    return lambda l: (l & ~6) | (((((l >> 1) & 3) + by) % 4) << 1)


def same_hop(l):
    return l ^ 64


def other_hop(l):
    return l ^ 65


def crossing(l):
    return l & 63 == 63


def onward_hop(l):
    if crossing(l):
        return (l + 1) % 128
    to = l ^ 65
    return to if to & 1 else (to + 2) % 128


def next_row(l):
    return l if l & 1 else (l + 2) % 128


def to_row(by):
    def to(l):
        if l & 1:
            return l
        y = (((l >> 1) & 3) + by) % 4
        there = (l & ~6) | (y << 1)
        return (there + 8) % 128 if y == 0 else there

    return to


def send(array, to, after=(), only=lambda l: True):
    if after:
        array = lax.optimization_barrier((array, *after))[0]
    return lax.ppermute(array, AXES, [(l, to(l)) for l in range(128) if only(l)])


VMEM = pl.BlockSpec(memory_space=pltpu.VMEM)
SMEM = pl.BlockSpec(memory_space=pltpu.SMEM)
ANY = pl.BlockSpec(memory_space=pl.ANY)


def params(mib):
    return pltpu.CompilerParams(vmem_limit_bytes=mib * 1024 * 1024)


def cost(flops, moved):
    return pl.CostEstimate(flops=flops, bytes_accessed=moved, transcendentals=0)


def mixed(ids, metric, pieces, slot, rows):
    left = jnp.concatenate(
        [metric[rows, pl.ds(pl.multiple_of(ids[k] * ROWS, ROWS), ROWS)] for _, _, k in pieces],
        axis=1,
    )
    right = jnp.concatenate([ref[n, slot] for ref, n, _ in pieces], axis=0)
    return jnp.dot(left, right, preferred_element_type=jnp.float32)


def tiles(count, tile):
    return [slice(t * tile, (t + 1) * tile) for t in range(count // tile)]


def transform(metric, ids, pieces, sofar=None, dtype=jnp.float32, tile=512):
    count = len(pieces)
    naux = metric.shape[0]
    nvir = pieces[0][0].shape[-1]
    given = [] if sofar is None else [sofar]
    arrays = []
    for array, _, _ in pieces:
        if not any(array is other for other in arrays):
            arrays.append(array)

    def kernel(ids, metric, *refs):
        out = refs[-1]
        listed = [
            (refs[next(i for i, other in enumerate(arrays) if other is array)], n, k)
            for array, n, k in pieces
        ]
        for slot in range(2):
            for rows in tiles(naux, tile):
                terms = mixed(ids, metric, listed, slot, rows)
                if given:
                    terms = terms + refs[len(arrays)][slot, rows]
                out[slot, rows] = terms.astype(dtype)

    return pl.pallas_call(
        kernel,
        out_shape=jax.ShapeDtypeStruct((2, naux, nvir), dtype),
        in_specs=[SMEM] + [VMEM] * (1 + len(arrays) + len(given)),
        out_specs=VMEM,
        input_output_aliases={2 + len(arrays): 0} if given and dtype == jnp.float32 else {},
        compiler_params=params(12),
        cost_estimate=cost(4 * naux * count * ROWS * nvir, 2 * naux * nvir),
        name="transform",
    )(ids, metric, *arrays, *given)


def finish_kernel(
    ids, ints, floats, metric, own_sum, before_sum, far, b2s, b2o, row, column, amps, density, before, left
):
    naux = metric.shape[0]
    for slot in range(2):
        for rows in tiles(naux, 512):
            terms = mixed(ids, metric, [(b2o, 0, 1)], slot, rows)
            before[slot, rows] = (terms + before_sum[slot, rows]).astype(jnp.bfloat16)
    pair_sum = column[...] + row[...]
    total = jnp.zeros(density.shape, jnp.float32)
    for slot in range(2):
        for rows in tiles(naux, 512):
            terms = mixed(ids, metric, [(b2s, 0, 0)], slot, rows)
            left[:, rows] = (terms + own_sum[slot, rows]).astype(jnp.bfloat16).T
        for rnd, rights in enumerate((before, far)):
            local = ints[slot, rnd]
            meet = jnp.dot(left[...], rights[local], preferred_element_type=jnp.float32)
            gap = pair_sum - floats[0, slot] - floats[1 + rnd, local]
            kept = ints[slot, 2 + rnd].astype(jnp.float32)
            amp = (kept * meet / gap).astype(jnp.bfloat16)
            amps[slot, rnd] = amp
            total = total + lax.dot_general(
                amp, amp, (((1,), (1,)), ((), ())), preferred_element_type=jnp.float32
            )
    density[...] = total.astype(jnp.bfloat16)


def finish(ids, ints, floats, metric, own, before, far, b2s, b2o, e_vir):
    _, naux, nvir = own.shape
    return pl.pallas_call(
        finish_kernel,
        out_shape=(
            jax.ShapeDtypeStruct((2, 2, nvir, nvir), jnp.bfloat16),
            jax.ShapeDtypeStruct((nvir, nvir), jnp.bfloat16),
            jax.ShapeDtypeStruct((2, naux, nvir), jnp.bfloat16),
        ),
        in_specs=[SMEM] * 3 + [VMEM] * 8,
        out_specs=(VMEM, VMEM, VMEM),
        scratch_shapes=[pltpu.VMEM((nvir, naux), jnp.bfloat16)],
        compiler_params=params(16),
        cost_estimate=cost(
            8 * naux * ROWS * nvir + 8 * naux * nvir * nvir + 8 * nvir**3, 8 * naux * nvir
        ),
        name="finish",
    )(ids, ints, floats, metric, own, before, far, b2s, b2o, e_vir[None, :], e_vir[:, None])


def gradient_of(ints, amps, before, far, upper=None, tile=256):
    _, naux, nvir = before.shape
    steps = naux // tile // 2
    first = 0 if upper is None else steps
    rest = () if upper is None else (upper,)

    def kernel(ints, amps, before, far, *refs):
        out, held, sems = refs[-3:]
        copies = []
        for step in range(steps):
            rows = slice((first + step) * tile, (first + step + 1) * tile)
            if step >= 2:
                copies[step - 2].wait()
            for slot in range(2):
                total = None
                for rnd, rights in enumerate((before, far)):
                    term = lax.dot_general(
                        rights[ints[slot, rnd], rows],
                        amps[slot, rnd],
                        (((1,), (1,)), ((), ())),
                        preferred_element_type=jnp.float32,
                    )
                    total = term if total is None else total + term
                held[step % 2, :, slot, :] = total.astype(jnp.bfloat16)
            copies.append(
                pltpu.make_async_copy(held.at[step % 2], out.at[rows], sems.at[step % 2])
            )
            copies[-1].start()
        for copy in copies[-2:]:
            copy.wait()

    return pl.pallas_call(
        kernel,
        out_shape=jax.ShapeDtypeStruct((naux, 2, nvir), jnp.bfloat16),
        in_specs=[SMEM, VMEM, VMEM, VMEM] + [ANY] * len(rest),
        out_specs=ANY,
        scratch_shapes=[
            pltpu.VMEM((2, tile, 2, nvir), jnp.bfloat16),
            pltpu.SemaphoreType.DMA((2,)),
        ],
        input_output_aliases={4: 0} if rest else {},
        compiler_params=params(12),
        cost_estimate=cost(4 * naux * nvir * nvir, 6 * naux * nvir),
        name="gradient",
    )(ints, amps, before, far, *rest)


def summed_at_owner(array):
    pieces = array.reshape(16, -1, array.shape[1])
    arrived = lax.all_to_all(pieces, "occ", split_axis=0, concat_axis=0, tiled=True)
    return arrived.astype(jnp.float32).sum(axis=0)


def summed_for_everyone(array):
    copies = jnp.broadcast_to(array[None], (8, *array.shape))
    arrived = lax.all_to_all(copies, "aux", 0, 0, tiled=True)
    return arrived.astype(jnp.float32).sum(axis=0)


def on_device(integrals, metric, e_occ, e_vir, partner, screen):
    nvir = integrals.shape[-1]
    device = lax.axis_index(AXES)
    aux = lax.axis_index("aux")
    y, x_hi = aux // 2, aux % 2

    by_owner = jnp.transpose(integrals, (1, 0, 2)).reshape(8, 2, ROWS, nvir)

    def block(index):
        return lax.dynamic_index_in_dim(by_owner, index, 0, True)

    def for_row(k):
        there = (y + k) % 4 * 2
        return block(there + x_hi), block(there + 1 - x_hi)

    order = jnp.array([0, 1, 3, 2], jnp.int32)
    here = (y - order) % 4 * 2
    own_ids = jnp.concatenate([here + x_hi, here + 1 - x_hi]).astype(jnp.int32)
    shifted = (here + 6 * (1 - x_hi)) % 8
    before_ids = jnp.concatenate([shifted + x_hi, shifted + 1 - x_hi]).astype(jnp.int32)

    same0, other0 = for_row(0)
    a0s = send(same0, same_hop)
    a0o = send(other0, other_hop)
    y1 = send(jnp.concatenate(for_row(1)), along_y(1))
    y3 = send(jnp.concatenate(for_row(3)), along_y(3))
    crosses = (device & 63) == 63

    def onward(mine, passing):
        return send(jnp.where(crosses, mine, passing), onward_hop)

    b0s = send(a0o, same_hop)
    b0o = onward(same0, a0s)
    third, here0, below0 = (
        jnp.concatenate(for_row(2)),
        block((y * 2 + 7) % 8),
        block((y * 2 + 5) % 8),
    )
    y1, y3, a0s, a0o, b0s, b0o, third, here0, below0 = lax.optimization_barrier(
        (y1, y3, a0s, a0o, b0s, b0o, third, here0, below0)
    )

    same1 = jnp.concatenate([y1[:1], y3[:1]])
    a1s = send(same1, same_hop)
    a1o = send(jnp.concatenate([y1[1:], y3[1:]]), other_hop)
    half = send(third, along_y(3))
    r1 = send(jnp.concatenate([other0, y1[1:]]), next_row)
    own = transform(metric, own_ids, [(same0, 0, 0), (y1, 0, 1), (y3, 0, 2), (b0s, 0, 4)])
    far = transform(metric, own_ids, [(a0s, 0, 0), (a0o, 0, 4)])
    a1s, a1o, half, r1, own, far = lax.optimization_barrier((a1s, a1o, half, r1, own, far))

    b1s = send(a1o, same_hop)
    b1o = onward(same1, a1s)
    y2 = send(half, along_y(3))
    far = transform(
        metric, own_ids, [(a1s, 0, 1), (a1s, 1, 2), (a1o, 0, 5), (a1o, 1, 6)], far
    )
    before = transform(metric, before_ids, [(r1, 0, 0), (r1, 1, 1), (b0o, 0, 4)])
    b1s, b1o, y2, far, before = lax.optimization_barrier((b1s, b1o, y2, far, before))

    a2s = send(y2[:1], same_hop)
    a2o = send(y2[1:], other_hop)
    near3 = send(below0, to_row(3), (), lambda l: l & 1 == 0)
    near0 = send(here0, to_row(0), (), lambda l: l & 1 == 0)
    own = transform(metric, own_ids, [(y2, 0, 3), (b1s, 0, 5), (b1s, 1, 6)], own)
    a2s, a2o, near0, near3, own = lax.optimization_barrier((a2s, a2o, near0, near3, own))

    b2s = send(a2o, same_hop)
    b2o = onward(y2[:1], a2s)
    near0 = jnp.where(x_hi == 0, near0, y3[1:])
    near3 = jnp.where(x_hi == 0, near3, y2[1:])
    before = transform(
        metric, before_ids, [(near0, 0, 2), (near3, 0, 3), (b1o, 0, 5), (b1o, 1, 6)], before
    )
    far = transform(metric, own_ids, [(a2s, 0, 3), (a2o, 0, 7)], far, jnp.bfloat16)

    ints = jnp.concatenate([partner, screen], axis=1).astype(jnp.int32)
    owners = jnp.stack([device, (device - 1) % 128, (device - 64) % 128])
    floats = e_occ[owners[:, None] * 2 + jnp.arange(2)[None, :]]
    ids = jnp.stack([own_ids[7], before_ids[7]])
    amps, density, before = finish(ids, ints, floats, metric, own, before, far, b2s, b2o, e_vir)
    rows = summed_at_owner(density).astype(jnp.bfloat16)
    gradient = gradient_of(ints, amps, before, far)
    rows, gradient = lax.optimization_barrier((rows, gradient))
    gradient = gradient_of(ints, amps, before, far, gradient)
    return gradient, summed_for_everyone(rows) / NOCC


def solution(mesh):
    placed = (P("aux", "occ", None), P(), P(), P(), P(AXES, None), P(AXES, None))
    return jax.shard_map(
        on_device,
        mesh=mesh,
        in_specs=placed,
        out_specs=(P(None, AXES, None), P("occ", None)),
        check_vma=False,
    )
```

```python
import jax
import jax.numpy as jnp
from jax import lax
from jax.experimental import pallas as pl
from jax.experimental.pallas import tpu as pltpu
from jax.sharding import PartitionSpec as P

NOCC = 256
AXES = ("occ", "aux")
ROWS = 256


def along_y(by):
    return lambda l: (l & ~6) | (((((l >> 1) & 3) + by) % 4) << 1)


def same_hop(l):
    return l ^ 64


def other_hop(l):
    return l ^ 65


def crossing(l):
    return l & 63 == 63


def onward_hop(l):
    if crossing(l):
        return (l + 1) % 128
    to = l ^ 65
    return to if to & 1 else (to + 2) % 128


def next_row(l):
    return l if l & 1 else (l + 2) % 128


def to_row(by):
    def to(l):
        if l & 1:
            return l
        y = (((l >> 1) & 3) + by) % 4
        there = (l & ~6) | (y << 1)
        return (there + 8) % 128 if y == 0 else there

    return to


def send(array, to, after=(), only=lambda l: True):
    if after:
        array = lax.optimization_barrier((array, *after))[0]
    return lax.ppermute(array, AXES, [(l, to(l)) for l in range(128) if only(l)])


VMEM = pl.BlockSpec(memory_space=pltpu.VMEM)
SMEM = pl.BlockSpec(memory_space=pltpu.SMEM)
HBM = pl.BlockSpec(memory_space=pltpu.HBM)


def params(mib):
    return pltpu.CompilerParams(vmem_limit_bytes=mib * 1024 * 1024)


def cost(flops, moved):
    return pl.CostEstimate(flops=flops, bytes_accessed=moved, transcendentals=0)


def mixed(ids, metric, pieces, slot, rows):
    left = jnp.concatenate(
        [metric[rows, pl.ds(pl.multiple_of(ids[k] * ROWS, ROWS), ROWS)] for _, _, k in pieces],
        axis=1,
    )
    right = jnp.concatenate([ref[n, slot] for ref, n, _ in pieces], axis=0)
    return jnp.dot(left, right, preferred_element_type=jnp.float32)


def tiles(count, tile):
    return [slice(t * tile, (t + 1) * tile) for t in range(count // tile)]


def transform(metric, ids, pieces, sofar=None, dtype=jnp.float32, tile=512):
    count = len(pieces)
    naux = metric.shape[0]
    nvir = pieces[0][0].shape[-1]
    given = [] if sofar is None else [sofar]
    arrays = []
    for array, _, _ in pieces:
        if not any(array is other for other in arrays):
            arrays.append(array)

    def kernel(ids, metric, *refs):
        out = refs[-1]
        listed = [
            (refs[next(i for i, other in enumerate(arrays) if other is array)], n, k)
            for array, n, k in pieces
        ]
        for slot in range(2):
            for rows in tiles(naux, tile):
                terms = mixed(ids, metric, listed, slot, rows)
                if given:
                    terms = terms + refs[len(arrays)][slot, rows]
                out[slot, rows] = terms.astype(dtype)

    return pl.pallas_call(
        kernel,
        out_shape=jax.ShapeDtypeStruct((2, naux, nvir), dtype),
        in_specs=[SMEM] + [VMEM] * (1 + len(arrays) + len(given)),
        out_specs=VMEM,
        input_output_aliases={2 + len(arrays): 0} if given and dtype == jnp.float32 else {},
        compiler_params=params(12),
        cost_estimate=cost(4 * naux * count * ROWS * nvir, 2 * naux * nvir),
        name="transform",
    )(ids, metric, *arrays, *given)


def finish_kernel(
    ids,
    ints,
    floats,
    metric_hbm,
    own_hbm,
    before_hbm,
    far_hbm,
    b2s,
    b2o,
    row,
    amps_out,
    density_out,
    before_out,
    metric,
    own_sum,
    before_sum,
    far,
    before,
    amps,
    density,
    left,
    sems,
    out_sems,
):
    naux = metric.shape[1]
    nvir = row.shape[1]
    routes = []
    for n in range(2):
        columns = pl.ds(pl.multiple_of(ids[1 - n] * ROWS, ROWS), ROWS)
        routes.append((metric_hbm.at[:, columns], metric.at[1 - n]))
    for slot in range(2):
        routes.append((before_hbm.at[slot], before_sum.at[slot]))
    routes += [
        (own_hbm.at[0], own_sum.at[0]),
        (far_hbm, far),
        (own_hbm.at[1], own_sum.at[1]),
    ]
    arriving = [
        pltpu.make_async_copy(source, target, sems.at[n])
        for n, (source, target) in enumerate(routes)
    ]
    for copy in arriving:
        copy.start()
    leaving = []

    def leave(source, target):
        leaving.append(pltpu.make_async_copy(source, target, out_sems.at[len(leaving)]))
        leaving[-1].start()

    def closed(n, piece, sums, slot, rows):
        terms = jnp.dot(metric[n, rows], piece[0, slot], preferred_element_type=jnp.float32)
        return (terms + sums[slot, rows]).astype(jnp.bfloat16)

    arriving[0].wait()
    for slot in range(2):
        arriving[2 + slot].wait()
        for rows in tiles(naux, 512):
            before[slot, rows] = closed(1, b2o, before_sum, slot, rows)
        leave(before.at[slot], before_out.at[slot])
    arriving[1].wait()
    column = jnp.broadcast_to(row[...], (128, nvir)).T[:, :1]
    pair_sum = column + row[...]
    total = jnp.zeros(density.shape, jnp.float32)
    for slot in range(2):
        arriving[4 + 2 * slot].wait()
        for rows in tiles(naux, 512):
            left[:, rows] = closed(0, b2s, own_sum, slot, rows).T
        for rnd, rights in enumerate((before, far)):
            if slot == 0 and rnd == 1:
                arriving[5].wait()
            local = ints[slot, rnd]
            meet = jnp.dot(left[...], rights[local], preferred_element_type=jnp.float32)
            gap = pair_sum - floats[0, slot] - floats[1 + rnd, local]
            kept = ints[slot, 2 + rnd].astype(jnp.float32)
            amp = (kept * meet / gap).astype(jnp.bfloat16)
            amps[slot, rnd] = amp
            total = total + lax.dot_general(
                amp, amp, (((1,), (1,)), ((), ())), preferred_element_type=jnp.float32
            )
        leave(amps.at[slot], amps_out.at[slot])
    density[...] = total.astype(jnp.bfloat16)
    leave(density, density_out)
    for copy in leaving:
        copy.wait()


def finish(ids, ints, floats, metric, own, before, far, b2s, b2o, row):
    _, naux, nvir = own.shape
    bf16 = jnp.bfloat16
    return pl.pallas_call(
        finish_kernel,
        out_shape=(
            jax.ShapeDtypeStruct((2, 2, nvir, nvir), bf16),
            jax.ShapeDtypeStruct((nvir, nvir), bf16),
            jax.ShapeDtypeStruct((2, naux, nvir), bf16),
        ),
        in_specs=[SMEM] * 3 + [HBM] * 4 + [VMEM] * 3,
        out_specs=(HBM, HBM, HBM),
        scratch_shapes=[
            pltpu.VMEM((2, naux, ROWS), bf16),
            pltpu.VMEM((2, naux, nvir), jnp.float32),
            pltpu.VMEM((2, naux, nvir), jnp.float32),
            pltpu.VMEM((2, naux, nvir), bf16),
            pltpu.VMEM((2, naux, nvir), bf16),
            pltpu.VMEM((2, 2, nvir, nvir), bf16),
            pltpu.VMEM((nvir, nvir), bf16),
            pltpu.VMEM((nvir, naux), bf16),
            pltpu.SemaphoreType.DMA((7,)),
            pltpu.SemaphoreType.DMA((5,)),
        ],
        compiler_params=params(58),
        cost_estimate=cost(
            8 * naux * ROWS * nvir + 8 * naux * nvir * nvir + 8 * nvir**3, 24 * naux * nvir
        ),
        name="finish",
    )(ids, ints, floats, metric, own, before, far, b2s, b2o, row)


def gradient_of(ints, amps, before, far, upper=None, tile=256):
    _, naux, nvir = before.shape
    steps = naux // tile // 2
    first = 0 if upper is None else steps
    rest = () if upper is None else (upper,)

    def kernel(ints, amps_hbm, before_hbm, far_hbm, *refs):
        out, amps, before, far, held, sems, out_sems = refs[-7:]
        ready = [pltpu.make_async_copy(amps_hbm, amps, sems.at[0])]
        for step in range(steps):
            there = slice((first + step) * tile, (first + step + 1) * tile)
            here = slice(step * tile, (step + 1) * tile)
            for n, (hbm, ref) in enumerate(((before_hbm, before), (far_hbm, far))):
                ready.append(
                    pltpu.make_async_copy(
                        hbm.at[:, there], ref.at[:, here], sems.at[1 + 2 * step + n]
                    )
                )
        for copy in ready:
            copy.start()
        ready[0].wait()
        copies = []
        for step in range(steps):
            there = slice((first + step) * tile, (first + step + 1) * tile)
            here = slice(step * tile, (step + 1) * tile)
            ready[1 + 2 * step].wait()
            ready[2 + 2 * step].wait()
            if step >= 2:
                copies[step - 2].wait()
            for slot in range(2):
                total = None
                for rnd, rights in enumerate((before, far)):
                    term = lax.dot_general(
                        rights[ints[slot, rnd], here],
                        amps[slot, rnd],
                        (((1,), (1,)), ((), ())),
                        preferred_element_type=jnp.float32,
                    )
                    total = term if total is None else total + term
                held[step % 2, :, slot, :] = total.astype(jnp.bfloat16)
            copies.append(
                pltpu.make_async_copy(held.at[step % 2], out.at[there], out_sems.at[step % 2])
            )
            copies[-1].start()
        for copy in copies[-2:]:
            copy.wait()

    bf16 = jnp.bfloat16
    return pl.pallas_call(
        kernel,
        out_shape=jax.ShapeDtypeStruct((naux, 2, nvir), bf16),
        in_specs=[SMEM, HBM, HBM, HBM] + [HBM] * len(rest),
        out_specs=HBM,
        scratch_shapes=[
            pltpu.VMEM((2, 2, nvir, nvir), bf16),
            pltpu.VMEM((2, naux // 2, nvir), bf16),
            pltpu.VMEM((2, naux // 2, nvir), bf16),
            pltpu.VMEM((2, tile, 2, nvir), bf16),
            pltpu.SemaphoreType.DMA((1 + 2 * steps,)),
            pltpu.SemaphoreType.DMA((2,)),
        ],
        input_output_aliases={4: 0} if rest else {},
        compiler_params=params(58),
        cost_estimate=cost(4 * naux * nvir * nvir, 6 * naux * nvir),
        name="gradient",
    )(ints, amps, before, far, *rest)


def summed_at_owner(array):
    pieces = array.reshape(16, -1, array.shape[1])
    arrived = lax.all_to_all(pieces, "occ", split_axis=0, concat_axis=0, tiled=True)
    return arrived.astype(jnp.float32).sum(axis=0)


def summed_for_everyone(array):
    copies = jnp.broadcast_to(array[None], (8, *array.shape))
    arrived = lax.all_to_all(copies, "aux", 0, 0, tiled=True)
    return arrived.astype(jnp.float32).sum(axis=0)


def on_device(integrals, metric, e_occ, e_vir, partner, screen):
    nvir = integrals.shape[-1]
    device = lax.axis_index(AXES)
    aux = lax.axis_index("aux")
    y, x_hi = aux // 2, aux % 2

    order = jnp.array([0, 1, 3, 2], jnp.int32)
    here = (y - order) % 4 * 2
    own_ids = jnp.concatenate([here + x_hi, here + 1 - x_hi]).astype(jnp.int32)
    shifted = (here + 6 * (1 - x_hi)) % 8
    before_ids = jnp.concatenate([shifted + x_hi, shifted + 1 - x_hi]).astype(jnp.int32)

    ints = jnp.concatenate([partner, screen], axis=1).astype(jnp.int32)
    owners = jnp.stack([device, (device - 1) % 128, (device - 64) % 128])
    floats = e_occ[owners[:, None] * 2 + jnp.arange(2)[None, :]]
    ids = jnp.stack([own_ids[7], before_ids[7]])
    even = x_hi == 0
    crosses = (device & 63) == 63
    row = e_vir[None, :]
    tables = (ints, floats, own_ids, before_ids, ids, row, even, crosses)
    integrals, tables = lax.optimization_barrier((integrals, tables))
    ints, floats, own_ids, before_ids, ids, row, even, crosses = tables

    by_owner = jnp.transpose(integrals, (1, 0, 2)).reshape(8, 2, ROWS, nvir)

    def block(index):
        return lax.dynamic_index_in_dim(by_owner, index, 0, True)

    def for_row(k):
        there = (y + k) % 4 * 2
        return block(there + x_hi), block(there + 1 - x_hi)

    same0, other0 = for_row(0)
    a0s = send(same0, same_hop)
    a0o = send(other0, other_hop)
    y1 = send(jnp.concatenate(for_row(1)), along_y(1))
    y3 = send(jnp.concatenate(for_row(3)), along_y(3))

    def onward(mine, passing):
        return send(jnp.where(crosses, mine, passing), onward_hop)

    b0s = send(a0o, same_hop)
    third, here0, below0 = (
        jnp.concatenate(for_row(2)),
        block((y * 2 + 7) % 8),
        block((y * 2 + 5) % 8),
    )
    y1, y3, a0s, a0o, b0s, third, here0, below0 = lax.optimization_barrier(
        (y1, y3, a0s, a0o, b0s, third, here0, below0)
    )

    same1 = jnp.concatenate([y1[:1], y3[:1]])
    a1s = send(same1, same_hop)
    a1o = send(jnp.concatenate([y1[1:], y3[1:]]), other_hop)
    half = send(third, along_y(3))
    b0o = onward(same0, a0s)
    r1 = send(jnp.concatenate([other0, y1[1:]]), next_row)
    own = transform(metric, own_ids, [(same0, 0, 0), (y1, 0, 1), (y3, 0, 2), (b0s, 0, 4)])
    far = transform(metric, own_ids, [(a0s, 0, 0), (a0o, 0, 4)])
    a1s, a1o, half, r1, b0o, own, far = lax.optimization_barrier(
        (a1s, a1o, half, r1, b0o, own, far)
    )

    b1s = send(a1o, same_hop)
    b1o = onward(same1, a1s)
    y2 = send(half, along_y(3))
    far = transform(
        metric, own_ids, [(a1s, 0, 1), (a1s, 1, 2), (a1o, 0, 5), (a1o, 1, 6)], far
    )
    before = transform(metric, before_ids, [(r1, 0, 0), (r1, 1, 1), (b0o, 0, 4)])
    b1s, b1o, y2, far, before = lax.optimization_barrier((b1s, b1o, y2, far, before))

    a2s = send(y2[:1], same_hop)
    a2o = send(y2[1:], other_hop)
    near3 = send(below0, to_row(3), (), lambda l: l & 1 == 0)
    near0 = send(here0, to_row(0), (), lambda l: l & 1 == 0)
    own = transform(metric, own_ids, [(y2, 0, 3), (b1s, 0, 5), (b1s, 1, 6)], own)
    a2s, a2o, near0, near3, own = lax.optimization_barrier((a2s, a2o, near0, near3, own))

    b2s = send(a2o, same_hop)
    b2o = onward(y2[:1], a2s)
    near0 = jnp.where(even, near0, y3[1:])
    near3 = jnp.where(even, near3, y2[1:])
    before = transform(
        metric, before_ids, [(near0, 0, 2), (near3, 0, 3), (b1o, 0, 5), (b1o, 1, 6)], before
    )
    far = transform(metric, own_ids, [(a2s, 0, 3), (a2o, 0, 7)], far, jnp.bfloat16)

    amps, density, before = finish(ids, ints, floats, metric, own, before, far, b2s, b2o, row)
    rows = summed_at_owner(density).astype(jnp.bfloat16)
    gradient = gradient_of(ints, amps, before, far)
    rows, gradient = lax.optimization_barrier((rows, gradient))
    gradient = gradient_of(ints, amps, before, far, gradient)
    return gradient, summed_for_everyone(rows) / NOCC


def solution(mesh):
    placed = (P("aux", "occ", None), P(), P(), P(), P(AXES, None), P(AXES, None))
    return jax.shard_map(
        on_device,
        mesh=mesh,
        in_specs=placed,
        out_specs=(P(None, AXES, None), P("occ", None)),
        check_vma=False,
    )
```

```python
import jax
import jax.numpy as jnp
from jax import lax
from jax.experimental import pallas as pl
from jax.experimental.pallas import tpu as pltpu
from jax.sharding import PartitionSpec as P

NOCC = 256
AXES = ("occ", "aux")
ROWS = 256


def along_y(by):
    return lambda l: (l & ~6) | (((((l >> 1) & 3) + by) % 4) << 1)


def same_hop(l):
    return l ^ 64


def other_hop(l):
    return l ^ 65


def crossing(l):
    return l & 63 == 63


def onward_hop(l):
    if crossing(l):
        return (l + 1) % 128
    to = l ^ 65
    return to if to & 1 else (to + 2) % 128


def next_row(l):
    return l if l & 1 else (l + 2) % 128


def to_row(by):
    def to(l):
        if l & 1:
            return l
        y = (((l >> 1) & 3) + by) % 4
        there = (l & ~6) | (y << 1)
        return (there + 8) % 128 if y == 0 else there

    return to


def send(array, to, after=(), only=lambda l: True):
    if after:
        array = lax.optimization_barrier((array, *after))[0]
    return lax.ppermute(array, AXES, [(l, to(l)) for l in range(128) if only(l)])


VMEM = pl.BlockSpec(memory_space=pltpu.VMEM)
SMEM = pl.BlockSpec(memory_space=pltpu.SMEM)
HBM = pl.BlockSpec(memory_space=pltpu.HBM)


def params(mib):
    return pltpu.CompilerParams(vmem_limit_bytes=mib * 1024 * 1024)


def cost(flops, moved):
    return pl.CostEstimate(flops=flops, bytes_accessed=moved, transcendentals=0)


def mixed(ids, metric, pieces, slot, rows):
    left = jnp.concatenate(
        [metric[rows, pl.ds(pl.multiple_of(ids[k] * ROWS, ROWS), ROWS)] for _, _, k in pieces],
        axis=1,
    )
    right = jnp.concatenate([ref[n, slot] for ref, n, _ in pieces], axis=0)
    return jnp.dot(left, right, preferred_element_type=jnp.float32)


def tiles(count, tile):
    return [slice(t * tile, (t + 1) * tile) for t in range(count // tile)]


def transform(metric, ids, pieces, sofar=None, dtype=jnp.float32, tile=512):
    count = len(pieces)
    naux = metric.shape[0]
    nvir = pieces[0][0].shape[-1]
    given = [] if sofar is None else [sofar]
    arrays = []
    for array, _, _ in pieces:
        if not any(array is other for other in arrays):
            arrays.append(array)

    def kernel(ids, metric, *refs):
        out = refs[-1]
        listed = [
            (refs[next(i for i, other in enumerate(arrays) if other is array)], n, k)
            for array, n, k in pieces
        ]
        for slot in range(2):
            for rows in tiles(naux, tile):
                terms = mixed(ids, metric, listed, slot, rows)
                if given:
                    terms = terms + refs[len(arrays)][slot, rows]
                out[slot, rows] = terms.astype(dtype)

    return pl.pallas_call(
        kernel,
        out_shape=jax.ShapeDtypeStruct((2, naux, nvir), dtype),
        in_specs=[SMEM] + [VMEM] * (1 + len(arrays) + len(given)),
        out_specs=VMEM,
        input_output_aliases={2 + len(arrays): 0} if given and dtype == jnp.float32 else {},
        compiler_params=params(12),
        cost_estimate=cost(4 * naux * count * ROWS * nvir, 2 * naux * nvir),
        name="transform",
    )(ids, metric, *arrays, *given)


def finish_kernel(
    ids,
    ints,
    floats,
    metric_hbm,
    own_hbm,
    before_hbm,
    far_hbm,
    b2s,
    b2o,
    row,
    amps_out,
    density_out,
    before_out,
    metric,
    own_sum,
    before_sum,
    far,
    before,
    amps,
    density,
    left,
    sems,
    out_sems,
):
    naux = metric.shape[1]
    nvir = row.shape[1]
    routes = []
    for n in range(2):
        columns = pl.ds(pl.multiple_of(ids[1 - n] * ROWS, ROWS), ROWS)
        routes.append((metric_hbm.at[:, columns], metric.at[1 - n]))
    for slot in range(2):
        routes.append((before_hbm.at[slot], before_sum.at[slot]))
    routes += [
        (own_hbm.at[0], own_sum.at[0]),
        (far_hbm, far),
        (own_hbm.at[1], own_sum.at[1]),
    ]
    arriving = [
        pltpu.make_async_copy(source, target, sems.at[n])
        for n, (source, target) in enumerate(routes)
    ]
    for copy in arriving:
        copy.start()
    leaving = []

    def leave(source, target):
        leaving.append(pltpu.make_async_copy(source, target, out_sems.at[len(leaving)]))
        leaving[-1].start()

    def closed(n, piece, sums, slot, rows):
        terms = jnp.dot(metric[n, rows], piece[0, slot], preferred_element_type=jnp.float32)
        return (terms + sums[slot, rows]).astype(jnp.bfloat16)

    arriving[0].wait()
    for slot in range(2):
        arriving[2 + slot].wait()
        for rows in tiles(naux, 512):
            before[slot, rows] = closed(1, b2o, before_sum, slot, rows)
        leave(before.at[slot], before_out.at[slot])
    arriving[1].wait()
    column = jnp.broadcast_to(row[...], (128, nvir)).T[:, :1]
    pair_sum = column + row[...]
    total = jnp.zeros(density.shape, jnp.float32)
    for slot in range(2):
        arriving[4 + 2 * slot].wait()
        for rows in tiles(naux, 512):
            left[:, rows] = closed(0, b2s, own_sum, slot, rows).T
        for rnd, rights in enumerate((before, far)):
            if slot == 0 and rnd == 1:
                arriving[5].wait()
            local = ints[slot, rnd]
            meet = jnp.dot(left[...], rights[local], preferred_element_type=jnp.float32)
            gap = pair_sum - floats[0, slot] - floats[1 + rnd, local]
            kept = ints[slot, 2 + rnd].astype(jnp.float32)
            amp = (kept * meet / gap).astype(jnp.bfloat16)
            amps[slot, rnd] = amp
            total = total + lax.dot_general(
                amp, amp, (((1,), (1,)), ((), ())), preferred_element_type=jnp.float32
            )
        leave(amps.at[slot], amps_out.at[slot])
    density[...] = total.astype(jnp.bfloat16)
    leave(density, density_out)
    for copy in leaving:
        copy.wait()


def finish(ids, ints, floats, metric, own, before, far, b2s, b2o, row):
    _, naux, nvir = own.shape
    bf16 = jnp.bfloat16
    return pl.pallas_call(
        finish_kernel,
        out_shape=(
            jax.ShapeDtypeStruct((2, 2, nvir, nvir), bf16),
            jax.ShapeDtypeStruct((nvir, nvir), bf16),
            jax.ShapeDtypeStruct((2, naux, nvir), bf16),
        ),
        in_specs=[SMEM] * 3 + [HBM] * 4 + [VMEM] * 3,
        out_specs=(HBM, HBM, HBM),
        scratch_shapes=[
            pltpu.VMEM((2, naux, ROWS), bf16),
            pltpu.VMEM((2, naux, nvir), jnp.float32),
            pltpu.VMEM((2, naux, nvir), jnp.float32),
            pltpu.VMEM((2, naux, nvir), bf16),
            pltpu.VMEM((2, naux, nvir), bf16),
            pltpu.VMEM((2, 2, nvir, nvir), bf16),
            pltpu.VMEM((nvir, nvir), bf16),
            pltpu.VMEM((nvir, naux), bf16),
            pltpu.SemaphoreType.DMA((7,)),
            pltpu.SemaphoreType.DMA((5,)),
        ],
        compiler_params=params(58),
        cost_estimate=cost(
            8 * naux * ROWS * nvir + 8 * naux * nvir * nvir + 8 * nvir**3, 24 * naux * nvir
        ),
        name="finish",
    )(ids, ints, floats, metric, own, before, far, b2s, b2o, row)


def gradient_of(ints, amps, before, far, upper=None, tile=256):
    _, naux, nvir = before.shape
    steps = naux // tile // 2
    first = 0 if upper is None else steps
    rest = () if upper is None else (upper,)

    def kernel(ints, amps_hbm, before_hbm, far_hbm, *refs):
        out, amps, before, far, held, sems, out_sems = refs[-7:]
        ready = [pltpu.make_async_copy(amps_hbm, amps, sems.at[0])]
        for step in range(steps):
            there = slice((first + step) * tile, (first + step + 1) * tile)
            here = slice(step * tile, (step + 1) * tile)
            for n, (hbm, ref) in enumerate(((before_hbm, before), (far_hbm, far))):
                ready.append(
                    pltpu.make_async_copy(
                        hbm.at[:, there], ref.at[:, here], sems.at[1 + 2 * step + n]
                    )
                )
        for copy in ready:
            copy.start()
        ready[0].wait()
        copies = []
        for step in range(steps):
            there = slice((first + step) * tile, (first + step + 1) * tile)
            here = slice(step * tile, (step + 1) * tile)
            ready[1 + 2 * step].wait()
            ready[2 + 2 * step].wait()
            if step >= 2:
                copies[step - 2].wait()
            for slot in range(2):
                total = None
                for rnd, rights in enumerate((before, far)):
                    term = lax.dot_general(
                        rights[ints[slot, rnd], here],
                        amps[slot, rnd],
                        (((1,), (1,)), ((), ())),
                        preferred_element_type=jnp.float32,
                    )
                    total = term if total is None else total + term
                held[step % 2, :, slot, :] = total.astype(jnp.bfloat16)
            copies.append(
                pltpu.make_async_copy(held.at[step % 2], out.at[there], out_sems.at[step % 2])
            )
            copies[-1].start()
        for copy in copies[-2:]:
            copy.wait()

    bf16 = jnp.bfloat16
    return pl.pallas_call(
        kernel,
        out_shape=jax.ShapeDtypeStruct((naux, 2, nvir), bf16),
        in_specs=[SMEM, HBM, HBM, HBM] + [HBM] * len(rest),
        out_specs=HBM,
        scratch_shapes=[
            pltpu.VMEM((2, 2, nvir, nvir), bf16),
            pltpu.VMEM((2, naux // 2, nvir), bf16),
            pltpu.VMEM((2, naux // 2, nvir), bf16),
            pltpu.VMEM((2, tile, 2, nvir), bf16),
            pltpu.SemaphoreType.DMA((1 + 2 * steps,)),
            pltpu.SemaphoreType.DMA((2,)),
        ],
        input_output_aliases={4: 0} if rest else {},
        compiler_params=params(58),
        cost_estimate=cost(4 * naux * nvir * nvir, 6 * naux * nvir),
        name="gradient",
    )(ints, amps, before, far, *rest)


def summed_at_owner(array):
    pieces = array.reshape(16, -1, array.shape[1])
    arrived = lax.all_to_all(pieces, "occ", split_axis=0, concat_axis=0, tiled=True)
    return arrived.astype(jnp.float32).sum(axis=0)


def summed_for_everyone(array):
    copies = jnp.broadcast_to(array[None], (8, *array.shape))
    arrived = lax.all_to_all(copies, "aux", 0, 0, tiled=True)
    return arrived.astype(jnp.float32).sum(axis=0)


def on_device(integrals, metric, e_occ, e_vir, partner, screen):
    nvir = integrals.shape[-1]
    device = lax.axis_index(AXES)
    aux = lax.axis_index("aux")
    y, x_hi = aux // 2, aux % 2

    order = jnp.array([0, 1, 3, 2], jnp.int32)
    here = (y - order) % 4 * 2
    own_ids = jnp.concatenate([here + x_hi, here + 1 - x_hi]).astype(jnp.int32)
    shifted = (here + 6 * (1 - x_hi)) % 8
    before_ids = jnp.concatenate([shifted + x_hi, shifted + 1 - x_hi]).astype(jnp.int32)

    ints = jnp.concatenate([partner, screen], axis=1).astype(jnp.int32)
    owners = jnp.stack([device, (device - 1) % 128, (device - 64) % 128])
    floats = e_occ[owners[:, None] * 2 + jnp.arange(2)[None, :]]
    ids = jnp.stack([own_ids[7], before_ids[7]])
    even = x_hi == 0
    crosses = (device & 63) == 63
    row = e_vir[None, :]
    tables = (ints, floats, own_ids, before_ids, ids, row, even, crosses)

    by_owner = jnp.transpose(integrals, (1, 0, 2)).reshape(8, 2, ROWS, nvir)

    def block(index):
        return lax.dynamic_index_in_dim(by_owner, index, 0, True)

    def for_row(k):
        there = (y + k) % 4 * 2
        return block(there + x_hi), block(there + 1 - x_hi)

    same0, other0 = for_row(0)
    a0s = send(same0, same_hop)
    a0o = send(other0, other_hop)
    y1 = send(jnp.concatenate(for_row(1)), along_y(1))
    y3 = send(jnp.concatenate(for_row(3)), along_y(3))
    b0s = send(a0o, same_hop)
    third, here0, below0 = (
        jnp.concatenate(for_row(2)),
        block((y * 2 + 7) % 8),
        block((y * 2 + 5) % 8),
    )
    y1, y3, a0s, a0o, b0s, third, here0, below0, tables = lax.optimization_barrier(
        (y1, y3, a0s, a0o, b0s, third, here0, below0, tables)
    )
    ints, floats, own_ids, before_ids, ids, row, even, crosses = tables

    same1 = jnp.concatenate([y1[:1], y3[:1]])
    a1s = send(same1, same_hop)
    a1o = send(jnp.concatenate([y1[1:], y3[1:]]), other_hop)
    half = send(third, along_y(3))
    r1 = send(jnp.concatenate([other0, y1[1:]]), next_row)
    own = transform(metric, own_ids, [(same0, 0, 0), (y1, 0, 1), (y3, 0, 2), (b0s, 0, 4)])
    far = transform(metric, own_ids, [(a0s, 0, 0), (a0o, 0, 4)])
    passing0 = jnp.where(crosses, same0, a0s)
    a1s, a1o, half, r1, passing0, own, far = lax.optimization_barrier(
        (a1s, a1o, half, r1, passing0, own, far)
    )

    b0o = send(passing0, onward_hop)
    b1o = send(jnp.where(crosses, same1, a1s), onward_hop)
    b1s = send(a1o, same_hop)
    y2 = send(half, along_y(3))
    far = transform(
        metric, own_ids, [(a1s, 0, 1), (a1s, 1, 2), (a1o, 0, 5), (a1o, 1, 6)], far
    )
    before = transform(metric, before_ids, [(r1, 0, 0), (r1, 1, 1)])
    b0o, b1s, b1o, y2, far, before = lax.optimization_barrier((b0o, b1s, b1o, y2, far, before))

    a2s = send(y2[:1], same_hop)
    a2o = send(y2[1:], other_hop)
    near3 = send(below0, to_row(3), (), lambda l: l & 1 == 0)
    near0 = send(here0, to_row(0), (), lambda l: l & 1 == 0)
    own = transform(
        metric, own_ids, [(y2, 0, 3), (b1s, 0, 5), (b1s, 1, 6)], own
    )
    before = transform(metric, before_ids, [(b0o, 0, 4), (b1o, 0, 5), (b1o, 1, 6)], before)
    a2s, a2o, near0, near3, own, before = lax.optimization_barrier(
        (a2s, a2o, near0, near3, own, before)
    )

    b2o = send(jnp.where(crosses, y2[:1], a2s), onward_hop)
    b2s = send(a2o, same_hop)
    near0 = jnp.where(even, near0, y3[1:])
    near3 = jnp.where(even, near3, y2[1:])
    far = transform(
        metric, own_ids, [(a2s, 0, 3), (a2o, 0, 7)], far, jnp.bfloat16
    )
    before = transform(
        metric, before_ids, [(near0, 0, 2), (near3, 0, 3)], before
    )

    amps, density, before = finish(ids, ints, floats, metric, own, before, far, b2s, b2o, row)
    rows = summed_at_owner(density).astype(jnp.bfloat16)
    gradient = gradient_of(ints, amps, before, far)
    rows, gradient = lax.optimization_barrier((rows, gradient))
    gradient = gradient_of(ints, amps, before, far, gradient)
    return gradient, summed_for_everyone(rows) / NOCC


def solution(mesh):
    placed = (P("aux", "occ", None), P(), P(), P(), P(AXES, None), P(AXES, None))
    return jax.shard_map(
        on_device,
        mesh=mesh,
        in_specs=placed,
        out_specs=(P(None, AXES, None), P("occ", None)),
        check_vma=False,
    )
```

```python
import jax
import jax.numpy as jnp
from jax import lax
from jax.experimental import pallas as pl
from jax.experimental.pallas import tpu as pltpu
from jax.sharding import PartitionSpec as P

NOCC = 256
AXES = ("occ", "aux")
ROWS = 256


def along_y(by):
    return lambda l: (l & ~6) | (((((l >> 1) & 3) + by) % 4) << 1)


def same_hop(l):
    return l ^ 64


def other_hop(l):
    return l ^ 65


def crossing(l):
    return l & 63 == 63


def onward_hop(l):
    if crossing(l):
        return (l + 1) % 128
    to = l ^ 65
    return to if to & 1 else (to + 2) % 128


def next_row(l):
    return l if l & 1 else (l + 2) % 128


def to_row(by):
    def to(l):
        if l & 1:
            return l
        y = (((l >> 1) & 3) + by) % 4
        there = (l & ~6) | (y << 1)
        return (there + 8) % 128 if y == 0 else there

    return to


def send(array, to, after=(), only=lambda l: True):
    if after:
        array = lax.optimization_barrier((array, *after))[0]
    return lax.ppermute(array, AXES, [(l, to(l)) for l in range(128) if only(l)])


VMEM = pl.BlockSpec(memory_space=pltpu.VMEM)
SMEM = pl.BlockSpec(memory_space=pltpu.SMEM)
HBM = pl.BlockSpec(memory_space=pltpu.HBM)


def params(mib):
    return pltpu.CompilerParams(vmem_limit_bytes=mib * 1024 * 1024)


def cost(flops, moved):
    return pl.CostEstimate(flops=flops, bytes_accessed=moved, transcendentals=0)


def mixed(ids, metric, pieces, slot, rows):
    left = jnp.concatenate(
        [metric[rows, pl.ds(pl.multiple_of(ids[k] * ROWS, ROWS), ROWS)] for _, _, k in pieces],
        axis=1,
    )
    right = jnp.concatenate([ref[n, slot] for ref, n, _ in pieces], axis=0)
    return jnp.dot(left, right, preferred_element_type=jnp.float32)


def tiles(count, tile):
    return [slice(t * tile, (t + 1) * tile) for t in range(count // tile)]


def transform(metric, ids, pieces, sofar=None, dtype=jnp.float32, tile=512):
    count = len(pieces)
    naux = metric.shape[0]
    nvir = pieces[0][0].shape[-1]
    given = [] if sofar is None else [sofar]
    arrays = []
    for array, _, _ in pieces:
        if not any(array is other for other in arrays):
            arrays.append(array)

    def kernel(ids, metric, *refs):
        out = refs[-1]
        listed = [
            (refs[next(i for i, other in enumerate(arrays) if other is array)], n, k)
            for array, n, k in pieces
        ]
        for slot in range(2):
            for rows in tiles(naux, tile):
                terms = mixed(ids, metric, listed, slot, rows)
                if given:
                    terms = terms + refs[len(arrays)][slot, rows]
                out[slot, rows] = terms.astype(dtype)

    return pl.pallas_call(
        kernel,
        out_shape=jax.ShapeDtypeStruct((2, naux, nvir), dtype),
        in_specs=[SMEM] + [VMEM] * (1 + len(arrays) + len(given)),
        out_specs=VMEM,
        input_output_aliases={2 + len(arrays): 0} if given and dtype == jnp.float32 else {},
        compiler_params=params(12),
        cost_estimate=cost(4 * naux * count * ROWS * nvir, 2 * naux * nvir),
        name="transform",
    )(ids, metric, *arrays, *given)


def finish_kernel(
    ids,
    ints,
    floats,
    metric_hbm,
    own_hbm,
    before_hbm,
    far_hbm,
    b2s,
    b2o,
    row,
    amps_out,
    density_out,
    before_out,
    metric,
    own_sum,
    before_sum,
    far,
    before,
    amps,
    density,
    left,
    sems,
    out_sems,
):
    naux = metric.shape[1]
    nvir = row.shape[1]
    routes = []
    for n in range(2):
        columns = pl.ds(pl.multiple_of(ids[1 - n] * ROWS, ROWS), ROWS)
        routes.append((metric_hbm.at[:, columns], metric.at[1 - n]))
    for slot in range(2):
        routes.append((before_hbm.at[slot], before_sum.at[slot]))
    routes += [
        (own_hbm.at[0], own_sum.at[0]),
        (far_hbm, far),
        (own_hbm.at[1], own_sum.at[1]),
    ]
    arriving = [
        pltpu.make_async_copy(source, target, sems.at[n])
        for n, (source, target) in enumerate(routes)
    ]
    for copy in arriving:
        copy.start()
    leaving = []

    def leave(source, target):
        leaving.append(pltpu.make_async_copy(source, target, out_sems.at[len(leaving)]))
        leaving[-1].start()

    def closed(n, piece, sums, slot, rows):
        terms = jnp.dot(metric[n, rows], piece[0, slot], preferred_element_type=jnp.float32)
        return (terms + sums[slot, rows]).astype(jnp.bfloat16)

    arriving[0].wait()
    for slot in range(2):
        arriving[2 + slot].wait()
        for rows in tiles(naux, 512):
            before[slot, rows] = closed(1, b2o, before_sum, slot, rows)
        leave(before.at[slot], before_out.at[slot])
    arriving[1].wait()
    column = jnp.broadcast_to(row[...], (128, nvir)).T[:, :1]
    pair_sum = column + row[...]
    total = jnp.zeros(density.shape, jnp.float32)
    for slot in range(2):
        arriving[4 + 2 * slot].wait()
        for rows in tiles(naux, 512):
            left[:, rows] = closed(0, b2s, own_sum, slot, rows).T
        for rnd, rights in enumerate((before, far)):
            if slot == 0 and rnd == 1:
                arriving[5].wait()
            local = ints[slot, rnd]
            meet = jnp.dot(left[...], rights[local], preferred_element_type=jnp.float32)
            gap = pair_sum - floats[0, slot] - floats[1 + rnd, local]
            kept = ints[slot, 2 + rnd].astype(jnp.float32)
            amp = (kept * meet / gap).astype(jnp.bfloat16)
            amps[slot, rnd] = amp
            total = total + lax.dot_general(
                amp, amp, (((1,), (1,)), ((), ())), preferred_element_type=jnp.float32
            )
        leave(amps.at[slot], amps_out.at[slot])
    density[...] = total.astype(jnp.bfloat16)
    leave(density, density_out)
    for copy in leaving:
        copy.wait()


def finish(ids, ints, floats, metric, own, before, far, b2s, b2o, row):
    _, naux, nvir = own.shape
    bf16 = jnp.bfloat16
    return pl.pallas_call(
        finish_kernel,
        out_shape=(
            jax.ShapeDtypeStruct((2, 2, nvir, nvir), bf16),
            jax.ShapeDtypeStruct((nvir, nvir), bf16),
            jax.ShapeDtypeStruct((2, naux, nvir), bf16),
        ),
        in_specs=[SMEM] * 3 + [HBM] * 4 + [VMEM] * 3,
        out_specs=(HBM, HBM, HBM),
        scratch_shapes=[
            pltpu.VMEM((2, naux, ROWS), bf16),
            pltpu.VMEM((2, naux, nvir), jnp.float32),
            pltpu.VMEM((2, naux, nvir), jnp.float32),
            pltpu.VMEM((2, naux, nvir), bf16),
            pltpu.VMEM((2, naux, nvir), bf16),
            pltpu.VMEM((2, 2, nvir, nvir), bf16),
            pltpu.VMEM((nvir, nvir), bf16),
            pltpu.VMEM((nvir, naux), bf16),
            pltpu.SemaphoreType.DMA((7,)),
            pltpu.SemaphoreType.DMA((5,)),
        ],
        compiler_params=params(58),
        cost_estimate=cost(
            8 * naux * ROWS * nvir + 8 * naux * nvir * nvir + 8 * nvir**3, 24 * naux * nvir
        ),
        name="finish",
    )(ids, ints, floats, metric, own, before, far, b2s, b2o, row)


def gradient_of(ints, amps, before, far, upper=None, tile=256):
    _, naux, nvir = before.shape
    steps = naux // tile // 2
    first = 0 if upper is None else steps
    rest = () if upper is None else (upper,)

    def kernel(ints, amps_hbm, before_hbm, far_hbm, *refs):
        out, amps, before, far, held, sems, out_sems = refs[-7:]
        ready = [pltpu.make_async_copy(amps_hbm, amps, sems.at[0])]
        for step in range(steps):
            there = slice((first + step) * tile, (first + step + 1) * tile)
            here = slice(step * tile, (step + 1) * tile)
            for n, (hbm, ref) in enumerate(((before_hbm, before), (far_hbm, far))):
                ready.append(
                    pltpu.make_async_copy(
                        hbm.at[:, there], ref.at[:, here], sems.at[1 + 2 * step + n]
                    )
                )
        for copy in ready:
            copy.start()
        ready[0].wait()
        copies = []
        for step in range(steps):
            there = slice((first + step) * tile, (first + step + 1) * tile)
            here = slice(step * tile, (step + 1) * tile)
            ready[1 + 2 * step].wait()
            ready[2 + 2 * step].wait()
            if step >= 2:
                copies[step - 2].wait()
            for slot in range(2):
                total = None
                for rnd, rights in enumerate((before, far)):
                    term = lax.dot_general(
                        rights[ints[slot, rnd], here],
                        amps[slot, rnd],
                        (((1,), (1,)), ((), ())),
                        preferred_element_type=jnp.float32,
                    )
                    total = term if total is None else total + term
                held[step % 2, :, slot, :] = total.astype(jnp.bfloat16)
            copies.append(
                pltpu.make_async_copy(held.at[step % 2], out.at[there], out_sems.at[step % 2])
            )
            copies[-1].start()
        for copy in copies[-2:]:
            copy.wait()

    bf16 = jnp.bfloat16
    return pl.pallas_call(
        kernel,
        out_shape=jax.ShapeDtypeStruct((naux, 2, nvir), bf16),
        in_specs=[SMEM, HBM, HBM, HBM] + [HBM] * len(rest),
        out_specs=HBM,
        scratch_shapes=[
            pltpu.VMEM((2, 2, nvir, nvir), bf16),
            pltpu.VMEM((2, naux // 2, nvir), bf16),
            pltpu.VMEM((2, naux // 2, nvir), bf16),
            pltpu.VMEM((2, tile, 2, nvir), bf16),
            pltpu.SemaphoreType.DMA((1 + 2 * steps,)),
            pltpu.SemaphoreType.DMA((2,)),
        ],
        input_output_aliases={4: 0} if rest else {},
        compiler_params=params(58),
        cost_estimate=cost(4 * naux * nvir * nvir, 6 * naux * nvir),
        name="gradient",
    )(ints, amps, before, far, *rest)


def summed_at_owner(array):
    pieces = array.reshape(16, -1, array.shape[1])
    arrived = lax.all_to_all(pieces, "occ", split_axis=0, concat_axis=0, tiled=True)
    return arrived.astype(jnp.float32).sum(axis=0)


def summed_for_everyone(array):
    copies = jnp.broadcast_to(array[None], (8, *array.shape))
    arrived = lax.all_to_all(copies, "aux", 0, 0, tiled=True)
    return arrived.astype(jnp.float32).sum(axis=0)


def on_device(integrals, metric, e_occ, e_vir, partner, screen):
    nvir = integrals.shape[-1]
    device = lax.axis_index(AXES)
    aux = lax.axis_index("aux")
    y, x_hi = aux // 2, aux % 2

    order = jnp.array([0, 1, 3, 2], jnp.int32)
    here = (y - order) % 4 * 2
    own_ids = jnp.concatenate([here + x_hi, here + 1 - x_hi]).astype(jnp.int32)
    shifted = (here + 6 * (1 - x_hi)) % 8
    before_ids = jnp.concatenate([shifted + x_hi, shifted + 1 - x_hi]).astype(jnp.int32)

    ints = jnp.concatenate([partner, screen], axis=1).astype(jnp.int32)
    owners = jnp.stack([device, (device - 1) % 128, (device - 64) % 128])
    floats = e_occ[owners[:, None] * 2 + jnp.arange(2)[None, :]]
    ids = jnp.stack([own_ids[7], before_ids[7]])
    even = x_hi == 0
    crosses = (device & 63) == 63
    row = e_vir[None, :]
    tables = (ints, floats, own_ids, before_ids, ids, row, even, crosses)

    by_owner = jnp.transpose(integrals, (1, 0, 2)).reshape(8, 2, ROWS, nvir)

    def block(index):
        return lax.dynamic_index_in_dim(by_owner, index, 0, True)

    def for_row(k, by_owner):
        return lax.dynamic_slice_in_dim(by_owner, (y + k) % 4 * 2, 2, 0)

    def same_of(pair):
        return jnp.where(even, pair[:1], pair[1:])

    def other_of(pair):
        return jnp.where(even, pair[1:], pair[:1])

    same0, other0 = block(y * 2 + x_hi), block(y * 2 + 1 - x_hi)
    a0s = send(same0, same_hop)
    a0o = send(other0, other_hop)
    y1 = send(for_row(1, by_owner), along_y(1))
    y3 = send(for_row(3, by_owner), along_y(3))
    a0s, a0o, by_owner = lax.optimization_barrier((a0s, a0o, by_owner))
    b0s = send(a0o, same_hop)
    third = for_row(2, by_owner)
    y1, y3, a0s, a0o, b0s, third, by_owner, tables = lax.optimization_barrier(
        (y1, y3, a0s, a0o, b0s, third, by_owner, tables)
    )
    ints, floats, own_ids, before_ids, ids, row, even, crosses = tables

    same1 = jnp.concatenate([same_of(y1), same_of(y3)])
    other1 = jnp.concatenate([other_of(y1), other_of(y3)])
    a1s = send(same1, same_hop)
    a1o = send(other1, other_hop)
    half = send(third, along_y(3))
    r1 = send(jnp.concatenate([other0, other_of(y1)]), next_row)
    here0, below0 = block((y * 2 + 7) % 8), block((y * 2 + 5) % 8)
    own = transform(
        metric, own_ids, [(same0, 0, 0), (same1, 0, 1), (same1, 1, 2), (b0s, 0, 4)]
    )
    far = transform(metric, own_ids, [(a0s, 0, 0), (a0o, 0, 4)])
    passing0 = jnp.where(crosses, same0, a0s)
    a1s, a1o, half, r1, passing0, own, far = lax.optimization_barrier(
        (a1s, a1o, half, r1, passing0, own, far)
    )

    b0o = send(passing0, onward_hop)
    b1o = send(jnp.where(crosses, same1, a1s), onward_hop)
    b1s = send(a1o, same_hop)
    y2 = send(half, along_y(3))
    far = transform(
        metric, own_ids, [(a1s, 0, 1), (a1s, 1, 2), (a1o, 0, 5), (a1o, 1, 6)], far
    )
    before = transform(metric, before_ids, [(r1, 0, 0), (r1, 1, 1)])
    b0o, b1s, b1o, y2, far, before = lax.optimization_barrier((b0o, b1s, b1o, y2, far, before))

    same2, other2 = same_of(y2), other_of(y2)
    a2s = send(same2, same_hop)
    a2o = send(other2, other_hop)
    near3 = send(below0, to_row(3), (), lambda l: l & 1 == 0)
    near0 = send(here0, to_row(0), (), lambda l: l & 1 == 0)
    own = transform(
        metric, own_ids, [(same2, 0, 3), (b1s, 0, 5), (b1s, 1, 6)], own
    )
    before = transform(metric, before_ids, [(b0o, 0, 4), (b1o, 0, 5), (b1o, 1, 6)], before)
    a2s, a2o, near0, near3, own, before = lax.optimization_barrier(
        (a2s, a2o, near0, near3, own, before)
    )

    b2o = send(jnp.where(crosses, same2, a2s), onward_hop)
    b2s = send(a2o, same_hop)
    near0 = jnp.where(even, near0, other1[1:])
    near3 = jnp.where(even, near3, other2)
    far = transform(
        metric, own_ids, [(a2s, 0, 3), (a2o, 0, 7)], far, jnp.bfloat16
    )
    before = transform(
        metric, before_ids, [(near0, 0, 2), (near3, 0, 3)], before
    )

    amps, density, before = finish(ids, ints, floats, metric, own, before, far, b2s, b2o, row)
    rows = summed_at_owner(density).astype(jnp.bfloat16)
    gradient = gradient_of(ints, amps, before, far)
    rows, gradient = lax.optimization_barrier((rows, gradient))
    gradient = gradient_of(ints, amps, before, far, gradient)
    return gradient, summed_for_everyone(rows) / NOCC


def solution(mesh):
    placed = (P("aux", "occ", None), P(), P(), P(), P(AXES, None), P(AXES, None))
    return jax.shard_map(
        on_device,
        mesh=mesh,
        in_specs=placed,
        out_specs=(P(None, AXES, None), P("occ", None)),
        check_vma=False,
    )
```

```python
import jax
import jax.numpy as jnp
from jax import lax
from jax.experimental import pallas as pl
from jax.experimental.pallas import tpu as pltpu
from jax.sharding import PartitionSpec as P

NOCC = 256
AXES = ("occ", "aux")
ROWS = 256


def along_y(by):
    return lambda l: (l & ~6) | (((((l >> 1) & 3) + by) % 4) << 1)


def same_hop(l):
    return l ^ 64


def other_hop(l):
    return l ^ 65


def crossing(l):
    return l & 63 == 63


def onward_hop(l):
    if crossing(l):
        return (l + 1) % 128
    to = l ^ 65
    return to if to & 1 else (to + 2) % 128


def next_row(l):
    return l if l & 1 else (l + 2) % 128


def to_row(by):
    def to(l):
        if l & 1:
            return l
        y = (((l >> 1) & 3) + by) % 4
        there = (l & ~6) | (y << 1)
        return (there + 8) % 128 if y == 0 else there

    return to


def send(array, to, after=(), only=lambda l: True):
    if after:
        array = lax.optimization_barrier((array, *after))[0]
    return lax.ppermute(array, AXES, [(l, to(l)) for l in range(128) if only(l)])


VMEM = pl.BlockSpec(memory_space=pltpu.VMEM)
SMEM = pl.BlockSpec(memory_space=pltpu.SMEM)
HBM = pl.BlockSpec(memory_space=pltpu.HBM)


def params(mib):
    return pltpu.CompilerParams(vmem_limit_bytes=mib * 1024 * 1024)


def cost(flops, moved):
    return pl.CostEstimate(flops=flops, bytes_accessed=moved, transcendentals=0)


def mixed(ids, metric, pieces, slot, rows):
    left = jnp.concatenate(
        [metric[rows, pl.ds(pl.multiple_of(ids[k] * ROWS, ROWS), ROWS)] for _, _, k in pieces],
        axis=1,
    )
    right = jnp.concatenate([ref[n, slot] for ref, n, _ in pieces], axis=0)
    return jnp.dot(left, right, preferred_element_type=jnp.float32)


def tiles(count, tile):
    return [slice(t * tile, (t + 1) * tile) for t in range(count // tile)]


def transform(metric, ids, pieces, sofar=None, dtype=jnp.float32, tile=512):
    count = len(pieces)
    naux = metric.shape[0]
    nvir = pieces[0][0].shape[-1]
    given = [] if sofar is None else [sofar]
    arrays = []
    for array, _, _ in pieces:
        if not any(array is other for other in arrays):
            arrays.append(array)

    def kernel(ids, metric, *refs):
        out = refs[-1]
        listed = [
            (refs[next(i for i, other in enumerate(arrays) if other is array)], n, k)
            for array, n, k in pieces
        ]
        for slot in range(2):
            for rows in tiles(naux, tile):
                terms = mixed(ids, metric, listed, slot, rows)
                if given:
                    terms = terms + refs[len(arrays)][slot, rows]
                out[slot, rows] = terms.astype(dtype)

    return pl.pallas_call(
        kernel,
        out_shape=jax.ShapeDtypeStruct((2, naux, nvir), dtype),
        in_specs=[SMEM] + [VMEM] * (1 + len(arrays) + len(given)),
        out_specs=VMEM,
        input_output_aliases={2 + len(arrays): 0} if given and dtype == jnp.float32 else {},
        compiler_params=params(12),
        cost_estimate=cost(4 * naux * count * ROWS * nvir, 2 * naux * nvir),
        name="transform",
    )(ids, metric, *arrays, *given)


def finish_kernel(
    ids,
    ints,
    floats,
    metric_hbm,
    own_hbm,
    before_hbm,
    far_hbm,
    b2s,
    b2o,
    row,
    amps_out,
    density_out,
    before_out,
    metric,
    own_sum,
    before_sum,
    far,
    before,
    amps,
    density,
    left,
    sems,
    out_sems,
):
    naux = metric.shape[1]
    nvir = row.shape[1]
    routes = []
    for n in range(2):
        columns = pl.ds(pl.multiple_of(ids[1 - n] * ROWS, ROWS), ROWS)
        routes.append((metric_hbm.at[:, columns], metric.at[1 - n]))
    for slot in range(2):
        routes.append((before_hbm.at[slot], before_sum.at[slot]))
    routes += [
        (own_hbm.at[0], own_sum.at[0]),
        (far_hbm, far),
        (own_hbm.at[1], own_sum.at[1]),
    ]
    arriving = [
        pltpu.make_async_copy(source, target, sems.at[n])
        for n, (source, target) in enumerate(routes)
    ]
    for copy in arriving:
        copy.start()
    leaving = []

    def leave(source, target):
        leaving.append(pltpu.make_async_copy(source, target, out_sems.at[len(leaving)]))
        leaving[-1].start()

    def closed(n, piece, sums, slot, rows):
        terms = jnp.dot(metric[n, rows], piece[0, slot], preferred_element_type=jnp.float32)
        return (terms + sums[slot, rows]).astype(jnp.bfloat16)

    arriving[0].wait()
    for slot in range(2):
        arriving[2 + slot].wait()
        for rows in tiles(naux, 512):
            before[slot, rows] = closed(1, b2o, before_sum, slot, rows)
        leave(before.at[slot], before_out.at[slot])
    arriving[1].wait()
    column = jnp.broadcast_to(row[...], (128, nvir)).T[:, :1]
    pair_sum = column + row[...]
    total = jnp.zeros(density.shape, jnp.float32)
    for slot in range(2):
        arriving[4 + 2 * slot].wait()
        for rows in tiles(naux, 512):
            left[:, rows] = closed(0, b2s, own_sum, slot, rows).T
        for rnd, rights in enumerate((before, far)):
            if slot == 0 and rnd == 1:
                arriving[5].wait()
            local = ints[slot, rnd]
            meet = jnp.dot(left[...], rights[local], preferred_element_type=jnp.float32)
            gap = pair_sum - floats[0, slot] - floats[1 + rnd, local]
            kept = ints[slot, 2 + rnd].astype(jnp.float32)
            amp = (kept * meet / gap).astype(jnp.bfloat16)
            amps[slot, rnd] = amp
            total = total + lax.dot_general(
                amp, amp, (((1,), (1,)), ((), ())), preferred_element_type=jnp.float32
            )
        leave(amps.at[slot], amps_out.at[slot])
    density[...] = total.astype(jnp.bfloat16)
    leave(density, density_out)
    for copy in leaving:
        copy.wait()


def finish(ids, ints, floats, metric, own, before, far, b2s, b2o, row):
    _, naux, nvir = own.shape
    bf16 = jnp.bfloat16
    return pl.pallas_call(
        finish_kernel,
        out_shape=(
            jax.ShapeDtypeStruct((2, 2, nvir, nvir), bf16),
            jax.ShapeDtypeStruct((nvir, nvir), bf16),
            jax.ShapeDtypeStruct((2, naux, nvir), bf16),
        ),
        in_specs=[SMEM] * 3 + [HBM] * 4 + [VMEM] * 3,
        out_specs=(HBM, HBM, HBM),
        scratch_shapes=[
            pltpu.VMEM((2, naux, ROWS), bf16),
            pltpu.VMEM((2, naux, nvir), jnp.float32),
            pltpu.VMEM((2, naux, nvir), jnp.float32),
            pltpu.VMEM((2, naux, nvir), bf16),
            pltpu.VMEM((2, naux, nvir), bf16),
            pltpu.VMEM((2, 2, nvir, nvir), bf16),
            pltpu.VMEM((nvir, nvir), bf16),
            pltpu.VMEM((nvir, naux), bf16),
            pltpu.SemaphoreType.DMA((7,)),
            pltpu.SemaphoreType.DMA((5,)),
        ],
        compiler_params=params(58),
        cost_estimate=cost(
            8 * naux * ROWS * nvir + 8 * naux * nvir * nvir + 8 * nvir**3, 24 * naux * nvir
        ),
        name="finish",
    )(ids, ints, floats, metric, own, before, far, b2s, b2o, row)


def gradient_of(ints, amps, before, far, upper=None, tile=256):
    _, naux, nvir = before.shape
    steps = naux // tile // 2
    first = 0 if upper is None else steps
    rest = () if upper is None else (upper,)

    def kernel(ints, amps_hbm, before_hbm, far_hbm, *refs):
        out, amps, before, far, held, sems, out_sems = refs[-7:]
        ready = [pltpu.make_async_copy(amps_hbm, amps, sems.at[0])]
        for step in range(steps):
            there = slice((first + step) * tile, (first + step + 1) * tile)
            here = slice(step * tile, (step + 1) * tile)
            for n, (hbm, ref) in enumerate(((before_hbm, before), (far_hbm, far))):
                ready.append(
                    pltpu.make_async_copy(
                        hbm.at[:, there], ref.at[:, here], sems.at[1 + 2 * step + n]
                    )
                )
        for copy in ready:
            copy.start()
        ready[0].wait()
        copies = []
        for step in range(steps):
            there = slice((first + step) * tile, (first + step + 1) * tile)
            here = slice(step * tile, (step + 1) * tile)
            ready[1 + 2 * step].wait()
            ready[2 + 2 * step].wait()
            if step >= 2:
                copies[step - 2].wait()
            for slot in range(2):
                total = None
                for rnd, rights in enumerate((before, far)):
                    term = lax.dot_general(
                        rights[ints[slot, rnd], here],
                        amps[slot, rnd],
                        (((1,), (1,)), ((), ())),
                        preferred_element_type=jnp.float32,
                    )
                    total = term if total is None else total + term
                held[step % 2, :, slot, :] = total.astype(jnp.bfloat16)
            copies.append(
                pltpu.make_async_copy(held.at[step % 2], out.at[there], out_sems.at[step % 2])
            )
            copies[-1].start()
        for copy in copies[-2:]:
            copy.wait()

    bf16 = jnp.bfloat16
    return pl.pallas_call(
        kernel,
        out_shape=jax.ShapeDtypeStruct((naux, 2, nvir), bf16),
        in_specs=[SMEM, HBM, HBM, HBM] + [HBM] * len(rest),
        out_specs=HBM,
        scratch_shapes=[
            pltpu.VMEM((2, 2, nvir, nvir), bf16),
            pltpu.VMEM((2, naux // 2, nvir), bf16),
            pltpu.VMEM((2, naux // 2, nvir), bf16),
            pltpu.VMEM((2, tile, 2, nvir), bf16),
            pltpu.SemaphoreType.DMA((1 + 2 * steps,)),
            pltpu.SemaphoreType.DMA((2,)),
        ],
        input_output_aliases={4: 0} if rest else {},
        compiler_params=params(58),
        cost_estimate=cost(4 * naux * nvir * nvir, 6 * naux * nvir),
        name="gradient",
    )(ints, amps, before, far, *rest)


def summed_at_owner(array):
    pieces = array.reshape(16, -1, array.shape[1])
    arrived = lax.all_to_all(pieces, "occ", split_axis=0, concat_axis=0, tiled=True)
    return arrived.astype(jnp.float32).sum(axis=0)


def summed_for_everyone(array):
    copies = jnp.broadcast_to(array[None], (8, *array.shape))
    arrived = lax.all_to_all(copies, "aux", 0, 0, tiled=True)
    return arrived.astype(jnp.float32).sum(axis=0)


def on_device(integrals, metric, e_occ, e_vir, partner, screen):
    nvir = integrals.shape[-1]
    device = lax.axis_index(AXES)
    aux = lax.axis_index("aux")
    y, x_hi = aux // 2, aux % 2

    order = jnp.array([0, 1, 3, 2], jnp.int32)
    here = (y - order) % 4 * 2
    own_ids = jnp.concatenate([here + x_hi, here + 1 - x_hi]).astype(jnp.int32)
    shifted = (here + 6 * (1 - x_hi)) % 8
    before_ids = jnp.concatenate([shifted + x_hi, shifted + 1 - x_hi]).astype(jnp.int32)

    ints = jnp.concatenate([partner, screen], axis=1).astype(jnp.int32)
    owners = jnp.stack([device, (device - 1) % 128, (device - 64) % 128])
    floats = e_occ[owners[:, None] * 2 + jnp.arange(2)[None, :]]
    ids = jnp.stack([own_ids[7], before_ids[7]])
    even = x_hi == 0
    crosses = (device & 63) == 63
    row = e_vir[None, :]
    tables = (ints, floats, own_ids, before_ids, ids, row, even, crosses)

    by_owner = jnp.transpose(integrals, (1, 0, 2)).reshape(8, 2, ROWS, nvir)

    def block(index):
        return lax.dynamic_index_in_dim(by_owner, index, 0, True)

    def for_row(k):
        there = (y + k) % 4 * 2
        return block(there + x_hi), block(there + 1 - x_hi)

    same0, other0 = for_row(0)
    a0s = send(same0, same_hop)
    a0o = send(other0, other_hop)
    y1 = send(jnp.concatenate(for_row(1)), along_y(1))
    y3 = send(jnp.concatenate(for_row(3)), along_y(3))
    third, here0, below0 = (
        jnp.concatenate(for_row(2)),
        block((y * 2 + 7) % 8),
        block((y * 2 + 5) % 8),
    )
    near0 = send(here0, to_row(0), (), lambda l: l & 1 == 0)
    y1, y3, a0s, a0o, near0, third, below0, tables = lax.optimization_barrier(
        (y1, y3, a0s, a0o, near0, third, below0, tables)
    )
    ints, floats, own_ids, before_ids, ids, row, even, crosses = tables

    same1 = jnp.concatenate([y1[:1], y3[:1]])
    a1s = send(same1, same_hop)
    a1o = send(jnp.concatenate([y1[1:], y3[1:]]), other_hop)
    half = send(third, along_y(3))
    r1 = send(jnp.concatenate([other0, y1[1:]]), next_row)
    own = transform(metric, own_ids, [(same0, 0, 0), (y1, 0, 1), (y3, 0, 2)])
    far = transform(metric, own_ids, [(a0s, 0, 0), (a0o, 0, 4)])
    passing0 = jnp.where(crosses, same0, a0s)
    a1s, a1o, half, r1, passing0, own, far = lax.optimization_barrier(
        (a1s, a1o, half, r1, passing0, own, far)
    )

    b0o = send(passing0, onward_hop)
    b1o = send(jnp.where(crosses, same1, a1s), onward_hop)
    b0s = send(a0o, same_hop)
    b1s = send(a1o, same_hop)
    y2 = send(half, along_y(3))
    far = transform(
        metric, own_ids, [(a1s, 0, 1), (a1s, 1, 2), (a1o, 0, 5), (a1o, 1, 6)], far
    )
    before = transform(metric, before_ids, [(r1, 0, 0), (r1, 1, 1)])
    y2, far, before = lax.optimization_barrier((y2, far, before))

    a2s = send(y2[:1], same_hop)
    a2o = send(y2[1:], other_hop)
    near3 = send(below0, to_row(3), (), lambda l: l & 1 == 0)
    own = transform(
        metric, own_ids, [(y2, 0, 3), (b0s, 0, 4), (b1s, 0, 5), (b1s, 1, 6)], own
    )
    before = transform(metric, before_ids, [(b0o, 0, 4), (b1o, 0, 5), (b1o, 1, 6)], before)
    a2s, a2o, near3, own, before = lax.optimization_barrier((a2s, a2o, near3, own, before))

    b2o = send(jnp.where(crosses, y2[:1], a2s), onward_hop)
    b2s = send(a2o, same_hop)
    near0 = jnp.where(even, near0, y3[1:])
    near3 = jnp.where(even, near3, y2[1:])
    far = transform(
        metric, own_ids, [(a2s, 0, 3), (a2o, 0, 7)], far, jnp.bfloat16
    )
    before = transform(
        metric, before_ids, [(near0, 0, 2), (near3, 0, 3)], before
    )

    amps, density, before = finish(ids, ints, floats, metric, own, before, far, b2s, b2o, row)
    rows = summed_at_owner(density).astype(jnp.bfloat16)
    gradient = gradient_of(ints, amps, before, far)
    rows, gradient = lax.optimization_barrier((rows, gradient))
    gradient = gradient_of(ints, amps, before, far, gradient)
    return gradient, summed_for_everyone(rows) / NOCC


def solution(mesh):
    placed = (P("aux", "occ", None), P(), P(), P(), P(AXES, None), P(AXES, None))
    return jax.shard_map(
        on_device,
        mesh=mesh,
        in_specs=placed,
        out_specs=(P(None, AXES, None), P("occ", None)),
        check_vma=False,
    )
```

```python
import jax
import jax.numpy as jnp
from jax import lax
from jax.experimental import pallas as pl
from jax.experimental.pallas import tpu as pltpu
from jax.sharding import PartitionSpec as P

NOCC = 256
AXES = ("occ", "aux")
ROWS = 256


def along_y(by):
    return lambda l: (l & ~6) | (((((l >> 1) & 3) + by) % 4) << 1)


def same_hop(l):
    return l ^ 64


def other_hop(l):
    return l ^ 65


def crossing(l):
    return l & 63 == 63


def onward_hop(l):
    if crossing(l):
        return (l + 1) % 128
    to = l ^ 65
    return to if to & 1 else (to + 2) % 128


def next_row(l):
    return l if l & 1 else (l + 2) % 128


def to_row(by):
    def to(l):
        if l & 1:
            return l
        y = (((l >> 1) & 3) + by) % 4
        there = (l & ~6) | (y << 1)
        return (there + 8) % 128 if y == 0 else there

    return to


def send(array, to, after=(), only=lambda l: True):
    if after:
        array = lax.optimization_barrier((array, *after))[0]
    return lax.ppermute(array, AXES, [(l, to(l)) for l in range(128) if only(l)])


VMEM = pl.BlockSpec(memory_space=pltpu.VMEM)
SMEM = pl.BlockSpec(memory_space=pltpu.SMEM)
HBM = pl.BlockSpec(memory_space=pltpu.HBM)


def params(mib):
    return pltpu.CompilerParams(vmem_limit_bytes=mib * 1024 * 1024)


def cost(flops, moved):
    return pl.CostEstimate(flops=flops, bytes_accessed=moved, transcendentals=0)


def mixed(ids, metric, pieces, slot, rows):
    left = jnp.concatenate(
        [metric[rows, pl.ds(pl.multiple_of(ids[k] * ROWS, ROWS), ROWS)] for _, _, k in pieces],
        axis=1,
    )
    right = jnp.concatenate([ref[n, slot] for ref, n, _ in pieces], axis=0)
    return jnp.dot(left, right, preferred_element_type=jnp.float32)


def tiles(count, tile):
    return [slice(t * tile, (t + 1) * tile) for t in range(count // tile)]


def transform(metric, ids, pieces, sofar=None, dtype=jnp.float32, tile=512):
    count = len(pieces)
    naux = metric.shape[0]
    nvir = pieces[0][0].shape[-1]
    given = [] if sofar is None else [sofar]
    arrays = []
    for array, _, _ in pieces:
        if not any(array is other for other in arrays):
            arrays.append(array)

    def kernel(ids, metric, *refs):
        out = refs[-1]
        listed = [
            (refs[next(i for i, other in enumerate(arrays) if other is array)], n, k)
            for array, n, k in pieces
        ]
        for slot in range(2):
            for rows in tiles(naux, tile):
                terms = mixed(ids, metric, listed, slot, rows)
                if given:
                    terms = terms + refs[len(arrays)][slot, rows]
                out[slot, rows] = terms.astype(dtype)

    return pl.pallas_call(
        kernel,
        out_shape=jax.ShapeDtypeStruct((2, naux, nvir), dtype),
        in_specs=[SMEM] + [VMEM] * (1 + len(arrays) + len(given)),
        out_specs=VMEM,
        input_output_aliases={2 + len(arrays): 0} if given and dtype == jnp.float32 else {},
        compiler_params=params(12),
        cost_estimate=cost(4 * naux * count * ROWS * nvir, 2 * naux * nvir),
        name="transform",
    )(ids, metric, *arrays, *given)


def finish_kernel(
    ids,
    ints,
    floats,
    metric_hbm,
    own_hbm,
    before_hbm,
    far_hbm,
    b2s,
    b2o,
    row,
    amps_out,
    density_out,
    before_out,
    metric,
    own_sum,
    before_sum,
    far,
    before,
    amps,
    density,
    left,
    sems,
    out_sems,
):
    naux = metric.shape[1]
    nvir = row.shape[1]
    routes = []
    for n in range(2):
        columns = pl.ds(pl.multiple_of(ids[1 - n] * ROWS, ROWS), ROWS)
        routes.append((metric_hbm.at[:, columns], metric.at[1 - n]))
    for slot in range(2):
        routes.append((before_hbm.at[slot], before_sum.at[slot]))
    routes += [
        (own_hbm.at[0], own_sum.at[0]),
        (far_hbm, far),
        (own_hbm.at[1], own_sum.at[1]),
    ]
    arriving = [
        pltpu.make_async_copy(source, target, sems.at[n])
        for n, (source, target) in enumerate(routes)
    ]
    for copy in arriving:
        copy.start()
    leaving = []

    def leave(source, target):
        leaving.append(pltpu.make_async_copy(source, target, out_sems.at[len(leaving)]))
        leaving[-1].start()

    def closed(n, piece, sums, slot, rows):
        terms = jnp.dot(metric[n, rows], piece[0, slot], preferred_element_type=jnp.float32)
        return (terms + sums[slot, rows]).astype(jnp.bfloat16)

    arriving[0].wait()
    for slot in range(2):
        arriving[2 + slot].wait()
        for rows in tiles(naux, 512):
            before[slot, rows] = closed(1, b2o, before_sum, slot, rows)
        leave(before.at[slot], before_out.at[slot])
    arriving[1].wait()
    column = jnp.broadcast_to(row[...], (128, nvir)).T[:, :1]
    pair_sum = column + row[...]
    total = jnp.zeros(density.shape, jnp.float32)
    for slot in range(2):
        arriving[4 + 2 * slot].wait()
        for rows in tiles(naux, 512):
            left[:, rows] = closed(0, b2s, own_sum, slot, rows).T
        for rnd, rights in enumerate((before, far)):
            if slot == 0 and rnd == 1:
                arriving[5].wait()
            local = ints[slot, rnd]
            meet = jnp.dot(left[...], rights[local], preferred_element_type=jnp.float32)
            gap = pair_sum - floats[0, slot] - floats[1 + rnd, local]
            kept = ints[slot, 2 + rnd].astype(jnp.float32)
            amp = (kept * meet / gap).astype(jnp.bfloat16)
            amps[slot, rnd] = amp
            total = total + lax.dot_general(
                amp, amp, (((1,), (1,)), ((), ())), preferred_element_type=jnp.float32
            )
        leave(amps.at[slot], amps_out.at[slot])
    density[...] = total.astype(jnp.bfloat16)
    leave(density, density_out)
    for copy in leaving:
        copy.wait()


def finish(ids, ints, floats, metric, own, before, far, b2s, b2o, row):
    _, naux, nvir = own.shape
    bf16 = jnp.bfloat16
    return pl.pallas_call(
        finish_kernel,
        out_shape=(
            jax.ShapeDtypeStruct((2, 2, nvir, nvir), bf16),
            jax.ShapeDtypeStruct((nvir, nvir), bf16),
            jax.ShapeDtypeStruct((2, naux, nvir), bf16),
        ),
        in_specs=[SMEM] * 3 + [HBM] * 4 + [VMEM] * 3,
        out_specs=(HBM, HBM, HBM),
        scratch_shapes=[
            pltpu.VMEM((2, naux, ROWS), bf16),
            pltpu.VMEM((2, naux, nvir), jnp.float32),
            pltpu.VMEM((2, naux, nvir), jnp.float32),
            pltpu.VMEM((2, naux, nvir), bf16),
            pltpu.VMEM((2, naux, nvir), bf16),
            pltpu.VMEM((2, 2, nvir, nvir), bf16),
            pltpu.VMEM((nvir, nvir), bf16),
            pltpu.VMEM((nvir, naux), bf16),
            pltpu.SemaphoreType.DMA((7,)),
            pltpu.SemaphoreType.DMA((5,)),
        ],
        compiler_params=params(58),
        cost_estimate=cost(
            8 * naux * ROWS * nvir + 8 * naux * nvir * nvir + 8 * nvir**3, 24 * naux * nvir
        ),
        name="finish",
    )(ids, ints, floats, metric, own, before, far, b2s, b2o, row)


def gradient_of(ints, amps, before, far, upper=None, tile=256):
    _, naux, nvir = before.shape
    steps = naux // tile // 2
    first = 0 if upper is None else steps
    rest = () if upper is None else (upper,)

    def kernel(ints, amps_hbm, before_hbm, far_hbm, *refs):
        out, amps, before, far, held, sems, out_sems = refs[-7:]
        ready = [pltpu.make_async_copy(amps_hbm, amps, sems.at[0])]
        for step in range(steps):
            there = slice((first + step) * tile, (first + step + 1) * tile)
            here = slice(step * tile, (step + 1) * tile)
            for n, (hbm, ref) in enumerate(((before_hbm, before), (far_hbm, far))):
                ready.append(
                    pltpu.make_async_copy(
                        hbm.at[:, there], ref.at[:, here], sems.at[1 + 2 * step + n]
                    )
                )
        for copy in ready:
            copy.start()
        ready[0].wait()
        copies = []
        for step in range(steps):
            there = slice((first + step) * tile, (first + step + 1) * tile)
            here = slice(step * tile, (step + 1) * tile)
            ready[1 + 2 * step].wait()
            ready[2 + 2 * step].wait()
            if step >= 2:
                copies[step - 2].wait()
            for slot in range(2):
                total = None
                for rnd, rights in enumerate((before, far)):
                    term = lax.dot_general(
                        rights[ints[slot, rnd], here],
                        amps[slot, rnd],
                        (((1,), (1,)), ((), ())),
                        preferred_element_type=jnp.float32,
                    )
                    total = term if total is None else total + term
                held[step % 2, :, slot, :] = total.astype(jnp.bfloat16)
            copies.append(
                pltpu.make_async_copy(held.at[step % 2], out.at[there], out_sems.at[step % 2])
            )
            copies[-1].start()
        for copy in copies[-2:]:
            copy.wait()

    bf16 = jnp.bfloat16
    return pl.pallas_call(
        kernel,
        out_shape=jax.ShapeDtypeStruct((naux, 2, nvir), bf16),
        in_specs=[SMEM, HBM, HBM, HBM] + [HBM] * len(rest),
        out_specs=HBM,
        scratch_shapes=[
            pltpu.VMEM((2, 2, nvir, nvir), bf16),
            pltpu.VMEM((2, naux // 2, nvir), bf16),
            pltpu.VMEM((2, naux // 2, nvir), bf16),
            pltpu.VMEM((2, tile, 2, nvir), bf16),
            pltpu.SemaphoreType.DMA((1 + 2 * steps,)),
            pltpu.SemaphoreType.DMA((2,)),
        ],
        input_output_aliases={4: 0} if rest else {},
        compiler_params=params(58),
        cost_estimate=cost(4 * naux * nvir * nvir, 6 * naux * nvir),
        name="gradient",
    )(ints, amps, before, far, *rest)


def summed_at_owner(array):
    pieces = array.reshape(16, -1, array.shape[1])
    arrived = lax.all_to_all(pieces, "occ", split_axis=0, concat_axis=0, tiled=True)
    return arrived.astype(jnp.float32).sum(axis=0)


def summed_for_everyone(array):
    copies = jnp.broadcast_to(array[None], (8, *array.shape))
    arrived = lax.all_to_all(copies, "aux", 0, 0, tiled=True)
    return arrived.astype(jnp.float32).sum(axis=0)


def on_device(integrals, metric, e_occ, e_vir, partner, screen):
    nvir = integrals.shape[-1]
    device = lax.axis_index(AXES)
    aux = lax.axis_index("aux")
    y, x_hi = aux // 2, aux % 2

    order = jnp.array([0, 1, 3, 2], jnp.int32)
    here = (y - order) % 4 * 2
    own_ids = jnp.concatenate([here + x_hi, here + 1 - x_hi]).astype(jnp.int32)
    shifted = (here + 6 * (1 - x_hi)) % 8
    before_ids = jnp.concatenate([shifted + x_hi, shifted + 1 - x_hi]).astype(jnp.int32)

    ints = jnp.concatenate([partner, screen], axis=1).astype(jnp.int32)
    owners = jnp.stack([device, (device - 1) % 128, (device - 64) % 128])
    floats = e_occ[owners[:, None] * 2 + jnp.arange(2)[None, :]]
    ids = jnp.stack([own_ids[7], before_ids[7]])
    even = x_hi == 0
    crosses = (device & 63) == 63
    row = e_vir[None, :]
    tables = (ints, floats, own_ids, before_ids, ids, row, even, crosses)

    by_owner = jnp.transpose(integrals, (1, 0, 2)).reshape(8, 2, ROWS, nvir)

    def block(index):
        return lax.dynamic_index_in_dim(by_owner, index, 0, True)

    def for_row(k):
        there = (y + k) % 4 * 2
        return block(there + x_hi), block(there + 1 - x_hi)

    even_only = lambda l: l & 1 == 0
    near0 = send(block((y * 2 + 7) % 8), to_row(0), (), even_only)
    y1 = send(jnp.concatenate(for_row(1)), along_y(1))
    y3 = send(jnp.concatenate(for_row(3)), along_y(3))
    near0, by_owner, same0, other0 = lax.optimization_barrier((near0, by_owner, *for_row(0)))
    a0s = send(same0, same_hop)
    a0o = send(other0, other_hop)
    third = jnp.concatenate(for_row(2))
    below0 = block((y * 2 + 5) % 8)
    y1, y3, a0s, a0o, near0, third, below0, tables = lax.optimization_barrier(
        (y1, y3, a0s, a0o, near0, third, below0, tables)
    )
    ints, floats, own_ids, before_ids, ids, row, even, crosses = tables

    same1 = jnp.concatenate([y1[:1], y3[:1]])
    a1s = send(same1, same_hop)
    a1o = send(jnp.concatenate([y1[1:], y3[1:]]), other_hop)
    half = send(third, along_y(3))
    r1 = send(jnp.concatenate([other0, y1[1:]]), next_row)
    near3 = send(below0, to_row(3), (), even_only)
    own = transform(metric, own_ids, [(same0, 0, 0), (y1, 0, 1), (y3, 0, 2)])
    far = transform(metric, own_ids, [(a0s, 0, 0), (a0o, 0, 4)])
    passing0 = jnp.where(crosses, same0, a0s)
    a1s, a1o, half, r1, near3, passing0, own, far = lax.optimization_barrier(
        (a1s, a1o, half, r1, near3, passing0, own, far)
    )

    b0o = send(passing0, onward_hop)
    b1o = send(jnp.where(crosses, same1, a1s), onward_hop)
    b0s = send(a0o, same_hop)
    b1s = send(a1o, same_hop)
    y2 = send(half, along_y(3))
    far = transform(
        metric, own_ids, [(a1s, 0, 1), (a1s, 1, 2), (a1o, 0, 5), (a1o, 1, 6)], far
    )
    before = transform(metric, before_ids, [(r1, 0, 0), (r1, 1, 1)])
    y2, far, before = lax.optimization_barrier((y2, far, before))

    a2s = send(y2[:1], same_hop)
    a2o = send(y2[1:], other_hop)
    own = transform(
        metric, own_ids, [(y2, 0, 3), (b0s, 0, 4), (b1s, 0, 5), (b1s, 1, 6)], own
    )
    before = transform(metric, before_ids, [(b0o, 0, 4), (b1o, 0, 5), (b1o, 1, 6)], before)
    a2s, a2o, own, before = lax.optimization_barrier((a2s, a2o, own, before))

    b2o = send(jnp.where(crosses, y2[:1], a2s), onward_hop)
    b2s = send(a2o, same_hop)
    near0 = jnp.where(even, near0, y3[1:])
    near3 = jnp.where(even, near3, y2[1:])
    far = transform(
        metric, own_ids, [(a2s, 0, 3), (a2o, 0, 7)], far, jnp.bfloat16
    )
    before = transform(
        metric, before_ids, [(near0, 0, 2), (near3, 0, 3)], before
    )

    amps, density, before = finish(ids, ints, floats, metric, own, before, far, b2s, b2o, row)
    rows = summed_at_owner(density).astype(jnp.bfloat16)
    gradient = gradient_of(ints, amps, before, far)
    rows, gradient = lax.optimization_barrier((rows, gradient))
    gradient = gradient_of(ints, amps, before, far, gradient)
    return gradient, summed_for_everyone(rows) / NOCC


def solution(mesh):
    placed = (P("aux", "occ", None), P(), P(), P(), P(AXES, None), P(AXES, None))
    return jax.shard_map(
        on_device,
        mesh=mesh,
        in_specs=placed,
        out_specs=(P(None, AXES, None), P("occ", None)),
        check_vma=False,
    )
```

```python
import jax
import jax.numpy as jnp
from jax import lax
from jax.experimental import pallas as pl
from jax.experimental.pallas import tpu as pltpu
from jax.sharding import PartitionSpec as P

NOCC = 256
AXES = ("occ", "aux")
ROWS = 256


def along_y(by):
    return lambda l: (l & ~6) | (((((l >> 1) & 3) + by) % 4) << 1)


def same_hop(l):
    return l ^ 64


def other_hop(l):
    return l ^ 65


def crossing(l):
    return l & 63 == 63


def onward_hop(l):
    if crossing(l):
        return (l + 1) % 128
    to = l ^ 65
    return to if to & 1 else (to + 2) % 128


def next_row(l):
    return l if l & 1 else (l + 2) % 128


def to_row(by):
    def to(l):
        if l & 1:
            return l
        y = (((l >> 1) & 3) + by) % 4
        there = (l & ~6) | (y << 1)
        return (there + 8) % 128 if y == 0 else there

    return to


def send(array, to, after=(), only=lambda l: True):
    if after:
        array = lax.optimization_barrier((array, *after))[0]
    return lax.ppermute(array, AXES, [(l, to(l)) for l in range(128) if only(l)])


VMEM = pl.BlockSpec(memory_space=pltpu.VMEM)
SMEM = pl.BlockSpec(memory_space=pltpu.SMEM)
HBM = pl.BlockSpec(memory_space=pltpu.HBM)


def params(mib):
    return pltpu.CompilerParams(vmem_limit_bytes=mib * 1024 * 1024)


def cost(flops, moved):
    return pl.CostEstimate(flops=flops, bytes_accessed=moved, transcendentals=0)


def mixed(ids, metric, pieces, slot, rows):
    left = jnp.concatenate(
        [metric[rows, pl.ds(pl.multiple_of(ids[k] * ROWS, ROWS), ROWS)] for _, _, k in pieces],
        axis=1,
    )
    right = jnp.concatenate([ref[n, slot] for ref, n, _ in pieces], axis=0)
    return jnp.dot(left, right, preferred_element_type=jnp.float32)


def tiles(count, tile):
    return [slice(t * tile, (t + 1) * tile) for t in range(count // tile)]


def transform(metric, ids, pieces, sofar=None, dtype=jnp.float32, tile=512):
    count = len(pieces)
    naux = metric.shape[0]
    nvir = pieces[0][0].shape[-1]
    given = [] if sofar is None else [sofar]
    arrays = []
    for array, _, _ in pieces:
        if not any(array is other for other in arrays):
            arrays.append(array)

    def kernel(ids, metric, *refs):
        out = refs[-1]
        listed = [
            (refs[next(i for i, other in enumerate(arrays) if other is array)], n, k)
            for array, n, k in pieces
        ]
        for slot in range(2):
            for rows in tiles(naux, tile):
                terms = mixed(ids, metric, listed, slot, rows)
                if given:
                    terms = terms + refs[len(arrays)][slot, rows]
                out[slot, rows] = terms.astype(dtype)

    return pl.pallas_call(
        kernel,
        out_shape=jax.ShapeDtypeStruct((2, naux, nvir), dtype),
        in_specs=[SMEM] + [VMEM] * (1 + len(arrays) + len(given)),
        out_specs=VMEM,
        input_output_aliases={2 + len(arrays): 0} if given and dtype == jnp.float32 else {},
        compiler_params=params(12),
        cost_estimate=cost(4 * naux * count * ROWS * nvir, 2 * naux * nvir),
        name="transform",
    )(ids, metric, *arrays, *given)


def finish_kernel(
    ids,
    ints,
    floats,
    metric_hbm,
    own_hbm,
    before_hbm,
    far_hbm,
    b2s,
    b2o,
    row,
    amps_out,
    density_out,
    before_out,
    metric,
    own_sum,
    before_sum,
    far,
    before,
    amps,
    density,
    left,
    sems,
    out_sems,
):
    naux = metric.shape[1]
    nvir = row.shape[1]
    routes = []
    for n in range(2):
        columns = pl.ds(pl.multiple_of(ids[1 - n] * ROWS, ROWS), ROWS)
        routes.append((metric_hbm.at[:, columns], metric.at[1 - n]))
    for slot in range(2):
        routes.append((before_hbm.at[slot], before_sum.at[slot]))
    routes += [
        (own_hbm.at[0], own_sum.at[0]),
        (far_hbm, far),
        (own_hbm.at[1], own_sum.at[1]),
    ]
    arriving = [
        pltpu.make_async_copy(source, target, sems.at[n])
        for n, (source, target) in enumerate(routes)
    ]
    for copy in arriving:
        copy.start()
    leaving = []

    def leave(source, target):
        leaving.append(pltpu.make_async_copy(source, target, out_sems.at[len(leaving)]))
        leaving[-1].start()

    def closed(n, piece, sums, slot, rows):
        terms = jnp.dot(metric[n, rows], piece[0, slot], preferred_element_type=jnp.float32)
        return (terms + sums[slot, rows]).astype(jnp.bfloat16)

    arriving[0].wait()
    for slot in range(2):
        arriving[2 + slot].wait()
        for rows in tiles(naux, 512):
            before[slot, rows] = closed(1, b2o, before_sum, slot, rows)
        leave(before.at[slot], before_out.at[slot])
    arriving[1].wait()
    column = jnp.broadcast_to(row[...], (128, nvir)).T[:, :1]
    pair_sum = column + row[...]
    total = jnp.zeros(density.shape, jnp.float32)
    for slot in range(2):
        arriving[4 + 2 * slot].wait()
        for rows in tiles(naux, 512):
            left[:, rows] = closed(0, b2s, own_sum, slot, rows).T
        for rnd, rights in enumerate((before, far)):
            if slot == 0 and rnd == 1:
                arriving[5].wait()
            local = ints[slot, rnd]
            meet = jnp.dot(left[...], rights[local], preferred_element_type=jnp.float32)
            gap = pair_sum - floats[0, slot] - floats[1 + rnd, local]
            kept = ints[slot, 2 + rnd].astype(jnp.float32)
            amp = (kept * meet / gap).astype(jnp.bfloat16)
            amps[slot, rnd] = amp
            total = total + lax.dot_general(
                amp, amp, (((1,), (1,)), ((), ())), preferred_element_type=jnp.float32
            )
        leave(amps.at[slot], amps_out.at[slot])
    density[...] = total.astype(jnp.bfloat16)
    leave(density, density_out)
    for copy in leaving:
        copy.wait()


def finish(ids, ints, floats, metric, own, before, far, b2s, b2o, row):
    _, naux, nvir = own.shape
    bf16 = jnp.bfloat16
    return pl.pallas_call(
        finish_kernel,
        out_shape=(
            jax.ShapeDtypeStruct((2, 2, nvir, nvir), bf16),
            jax.ShapeDtypeStruct((nvir, nvir), bf16),
            jax.ShapeDtypeStruct((2, naux, nvir), bf16),
        ),
        in_specs=[SMEM] * 3 + [HBM] * 4 + [VMEM] * 3,
        out_specs=(HBM, HBM, HBM),
        scratch_shapes=[
            pltpu.VMEM((2, naux, ROWS), bf16),
            pltpu.VMEM((2, naux, nvir), jnp.float32),
            pltpu.VMEM((2, naux, nvir), jnp.float32),
            pltpu.VMEM((2, naux, nvir), bf16),
            pltpu.VMEM((2, naux, nvir), bf16),
            pltpu.VMEM((2, 2, nvir, nvir), bf16),
            pltpu.VMEM((nvir, nvir), bf16),
            pltpu.VMEM((nvir, naux), bf16),
            pltpu.SemaphoreType.DMA((7,)),
            pltpu.SemaphoreType.DMA((5,)),
        ],
        compiler_params=params(58),
        cost_estimate=cost(
            8 * naux * ROWS * nvir + 8 * naux * nvir * nvir + 8 * nvir**3, 24 * naux * nvir
        ),
        name="finish",
    )(ids, ints, floats, metric, own, before, far, b2s, b2o, row)


def gradient_of(ints, amps, before, far, upper=None, tile=256):
    _, naux, nvir = before.shape
    steps = naux // tile // 2
    first = 0 if upper is None else steps
    rest = () if upper is None else (upper,)

    def kernel(ints, amps_hbm, before_hbm, far_hbm, *refs):
        out, amps, before, far, held, sems, out_sems = refs[-7:]
        ready = [pltpu.make_async_copy(amps_hbm, amps, sems.at[0])]
        for step in range(steps):
            there = slice((first + step) * tile, (first + step + 1) * tile)
            here = slice(step * tile, (step + 1) * tile)
            for n, (hbm, ref) in enumerate(((before_hbm, before), (far_hbm, far))):
                ready.append(
                    pltpu.make_async_copy(
                        hbm.at[:, there], ref.at[:, here], sems.at[1 + 2 * step + n]
                    )
                )
        for copy in ready:
            copy.start()
        ready[0].wait()
        copies = []
        for step in range(steps):
            there = slice((first + step) * tile, (first + step + 1) * tile)
            here = slice(step * tile, (step + 1) * tile)
            ready[1 + 2 * step].wait()
            ready[2 + 2 * step].wait()
            if step >= 2:
                copies[step - 2].wait()
            for slot in range(2):
                total = None
                for rnd, rights in enumerate((before, far)):
                    term = lax.dot_general(
                        rights[ints[slot, rnd], here],
                        amps[slot, rnd],
                        (((1,), (1,)), ((), ())),
                        preferred_element_type=jnp.float32,
                    )
                    total = term if total is None else total + term
                held[step % 2, :, slot, :] = total.astype(jnp.bfloat16)
            copies.append(
                pltpu.make_async_copy(held.at[step % 2], out.at[there], out_sems.at[step % 2])
            )
            copies[-1].start()
        for copy in copies[-2:]:
            copy.wait()

    bf16 = jnp.bfloat16
    return pl.pallas_call(
        kernel,
        out_shape=jax.ShapeDtypeStruct((naux, 2, nvir), bf16),
        in_specs=[SMEM, HBM, HBM, HBM] + [HBM] * len(rest),
        out_specs=HBM,
        scratch_shapes=[
            pltpu.VMEM((2, 2, nvir, nvir), bf16),
            pltpu.VMEM((2, naux // 2, nvir), bf16),
            pltpu.VMEM((2, naux // 2, nvir), bf16),
            pltpu.VMEM((2, tile, 2, nvir), bf16),
            pltpu.SemaphoreType.DMA((1 + 2 * steps,)),
            pltpu.SemaphoreType.DMA((2,)),
        ],
        input_output_aliases={4: 0} if rest else {},
        compiler_params=params(58),
        cost_estimate=cost(4 * naux * nvir * nvir, 6 * naux * nvir),
        name="gradient",
    )(ints, amps, before, far, *rest)


def summed_at_owner(array):
    pieces = array.reshape(16, -1, array.shape[1])
    arrived = lax.all_to_all(pieces, "occ", split_axis=0, concat_axis=0, tiled=True)
    return arrived.astype(jnp.float32).sum(axis=0)


def summed_for_everyone(array):
    copies = jnp.broadcast_to(array[None], (8, *array.shape))
    arrived = lax.all_to_all(copies, "aux", 0, 0, tiled=True)
    return arrived.astype(jnp.float32).sum(axis=0)


def on_device(integrals, metric, e_occ, e_vir, partner, screen):
    nvir = integrals.shape[-1]
    device = lax.axis_index(AXES)
    aux = lax.axis_index("aux")
    y, x_hi = aux // 2, aux % 2

    order = jnp.array([0, 1, 3, 2], jnp.int32)
    here = (y - order) % 4 * 2
    own_ids = jnp.concatenate([here + x_hi, here + 1 - x_hi]).astype(jnp.int32)
    shifted = (here + 6 * (1 - x_hi)) % 8
    before_ids = jnp.concatenate([shifted + x_hi, shifted + 1 - x_hi]).astype(jnp.int32)

    ints = jnp.concatenate([partner, screen], axis=1).astype(jnp.int32)
    owners = jnp.stack([device, (device - 1) % 128, (device - 64) % 128])
    floats = e_occ[owners[:, None] * 2 + jnp.arange(2)[None, :]]
    ids = jnp.stack([own_ids[7], before_ids[7]])
    even = x_hi == 0
    crosses = (device & 63) == 63
    row = e_vir[None, :]
    tables = (ints, floats, own_ids, before_ids, ids, row, even, crosses)

    by_owner = jnp.transpose(integrals, (1, 0, 2)).reshape(8, 2, ROWS, nvir)

    def block(index):
        return lax.dynamic_index_in_dim(by_owner, index, 0, True)

    def for_row(k):
        there = (y + k) % 4 * 2
        return block(there + x_hi), block(there + 1 - x_hi)

    even_only = lambda l: l & 1 == 0
    near0 = send(block((y * 2 + 7) % 8), to_row(0), (), even_only)
    y1 = send(jnp.concatenate(for_row(1)), along_y(1))
    y3 = send(jnp.concatenate(for_row(3)), along_y(3))
    near0, by_owner, same0, other0 = lax.optimization_barrier((near0, by_owner, *for_row(0)))
    a0s = send(same0, same_hop)
    a0o = send(other0, other_hop)
    third = jnp.concatenate(for_row(2))
    below0 = block((y * 2 + 5) % 8)
    y1, y3, a0s, a0o, near0, third, below0, tables = lax.optimization_barrier(
        (y1, y3, a0s, a0o, near0, third, below0, tables)
    )
    ints, floats, own_ids, before_ids, ids, row, even, crosses = tables

    same1 = jnp.concatenate([y1[:1], y3[:1]])
    a1s = send(same1, same_hop)
    a1o = send(jnp.concatenate([y1[1:], y3[1:]]), other_hop)
    half = send(third, along_y(3))
    r1 = send(jnp.concatenate([other0, y1[1:]]), next_row)
    near3 = send(below0, to_row(3), (), even_only)
    own = transform(metric, own_ids, [(same0, 0, 0), (y1, 0, 1), (y3, 0, 2)])
    far = transform(metric, own_ids, [(a0s, 0, 0), (a0o, 0, 4)])
    passing0 = jnp.where(crosses, same0, a0s)
    a1s, a1o, half, r1, near3, passing0, own, far = lax.optimization_barrier(
        (a1s, a1o, half, r1, near3, passing0, own, far)
    )

    passing = jnp.concatenate([passing0, jnp.where(crosses, same1, a1s)])
    b1o = send(passing, onward_hop)
    b0s = send(a0o, same_hop)
    b1s = send(a1o, same_hop)
    y2 = send(half, along_y(3))
    far = transform(
        metric, own_ids, [(a1s, 0, 1), (a1s, 1, 2), (a1o, 0, 5), (a1o, 1, 6)], far
    )
    before = transform(metric, before_ids, [(r1, 0, 0), (r1, 1, 1)])
    y2, y3, near0, near3, far, before = lax.optimization_barrier(
        (y2, y3, near0, near3, far, before)
    )

    a2s = send(y2[:1], same_hop)
    a2o = send(y2[1:], other_hop)
    own = transform(
        metric, own_ids, [(y2, 0, 3), (b0s, 0, 4), (b1s, 0, 5), (b1s, 1, 6)], own
    )
    before = transform(metric, before_ids, [(b1o, 0, 4), (b1o, 1, 5), (b1o, 2, 6)], before)
    a2s, a2o, y3, near0, near3, own, before = lax.optimization_barrier(
        (a2s, a2o, y3, near0, near3, own, before)
    )

    b2o = send(jnp.where(crosses, y2[:1], a2s), onward_hop)
    b2s = send(a2o, same_hop)
    near0 = jnp.where(even, near0, y3[1:])
    near3 = jnp.where(even, near3, y2[1:])
    far = transform(
        metric, own_ids, [(a2s, 0, 3), (a2o, 0, 7)], far, jnp.bfloat16
    )
    before = transform(
        metric, before_ids, [(near0, 0, 2), (near3, 0, 3)], before
    )

    amps, density, before = finish(ids, ints, floats, metric, own, before, far, b2s, b2o, row)
    rows = summed_at_owner(density).astype(jnp.bfloat16)
    gradient = gradient_of(ints, amps, before, far)
    rows, gradient = lax.optimization_barrier((rows, gradient))
    gradient = gradient_of(ints, amps, before, far, gradient)
    return gradient, summed_for_everyone(rows) / NOCC


def solution(mesh):
    placed = (P("aux", "occ", None), P(), P(), P(), P(AXES, None), P(AXES, None))
    return jax.shard_map(
        on_device,
        mesh=mesh,
        in_specs=placed,
        out_specs=(P(None, AXES, None), P("occ", None)),
        check_vma=False,
    )
```

```python
import jax
import jax.numpy as jnp
from jax import lax
from jax.experimental import pallas as pl
from jax.experimental.pallas import tpu as pltpu
from jax.sharding import PartitionSpec as P

NOCC = 256
AXES = ("occ", "aux")
ROWS = 256


def along_y(by):
    return lambda l: (l & ~6) | (((((l >> 1) & 3) + by) % 4) << 1)


def same_hop(l):
    return l ^ 64


def other_hop(l):
    return l ^ 65


def crossing(l):
    return l & 63 == 63


def onward_hop(l):
    if crossing(l):
        return (l + 1) % 128
    to = l ^ 65
    return to if to & 1 else (to + 2) % 128


def next_row(l):
    return l if l & 1 else (l + 2) % 128


def to_row(by):
    def to(l):
        if l & 1:
            return l
        y = (((l >> 1) & 3) + by) % 4
        there = (l & ~6) | (y << 1)
        return (there + 8) % 128 if y == 0 else there

    return to


def send(array, to, after=(), only=lambda l: True):
    if after:
        array = lax.optimization_barrier((array, *after))[0]
    return lax.ppermute(array, AXES, [(l, to(l)) for l in range(128) if only(l)])


VMEM = pl.BlockSpec(memory_space=pltpu.VMEM)
SMEM = pl.BlockSpec(memory_space=pltpu.SMEM)
HBM = pl.BlockSpec(memory_space=pltpu.HBM)


def params(mib):
    return pltpu.CompilerParams(vmem_limit_bytes=mib * 1024 * 1024)


def cost(flops, moved):
    return pl.CostEstimate(flops=flops, bytes_accessed=moved, transcendentals=0)


def mixed(ids, metric, pieces, slot, rows):
    left = jnp.concatenate(
        [metric[rows, pl.ds(pl.multiple_of(ids[k] * ROWS, ROWS), ROWS)] for _, _, k in pieces],
        axis=1,
    )
    right = jnp.concatenate([ref[n, slot] for ref, n, _ in pieces], axis=0)
    return jnp.dot(left, right, preferred_element_type=jnp.float32)


def tiles(count, tile):
    return [slice(t * tile, (t + 1) * tile) for t in range(count // tile)]


def transform(metric, ids, pieces, sofar=None, dtype=jnp.float32, tile=512):
    count = len(pieces)
    naux = metric.shape[0]
    nvir = pieces[0][0].shape[-1]
    given = [] if sofar is None else [sofar]
    arrays = []
    for array, _, _ in pieces:
        if not any(array is other for other in arrays):
            arrays.append(array)

    def kernel(ids, metric, *refs):
        out = refs[-1]
        listed = [
            (refs[next(i for i, other in enumerate(arrays) if other is array)], n, k)
            for array, n, k in pieces
        ]
        for slot in range(2):
            for rows in tiles(naux, tile):
                terms = mixed(ids, metric, listed, slot, rows)
                if given:
                    terms = terms + refs[len(arrays)][slot, rows]
                out[slot, rows] = terms.astype(dtype)

    return pl.pallas_call(
        kernel,
        out_shape=jax.ShapeDtypeStruct((2, naux, nvir), dtype),
        in_specs=[SMEM] + [VMEM] * (1 + len(arrays) + len(given)),
        out_specs=VMEM,
        input_output_aliases={2 + len(arrays): 0} if given and dtype == jnp.float32 else {},
        compiler_params=params(12),
        cost_estimate=cost(4 * naux * count * ROWS * nvir, 2 * naux * nvir),
        name="transform",
    )(ids, metric, *arrays, *given)


def finish_kernel(
    ids,
    ints,
    floats,
    metric_hbm,
    own_hbm,
    before_hbm,
    far_hbm,
    b2s,
    b2o,
    row,
    amps_out,
    density_out,
    before_out,
    metric,
    own_sum,
    before_sum,
    far,
    before,
    amps,
    density,
    left,
    sems,
    out_sems,
):
    naux = metric.shape[1]
    nvir = row.shape[1]
    routes = []
    for n in range(2):
        columns = pl.ds(pl.multiple_of(ids[1 - n] * ROWS, ROWS), ROWS)
        routes.append((metric_hbm.at[:, columns], metric.at[1 - n]))
    for slot in range(2):
        routes.append((before_hbm.at[slot], before_sum.at[slot]))
    routes += [
        (own_hbm.at[0], own_sum.at[0]),
        (far_hbm, far),
        (own_hbm.at[1], own_sum.at[1]),
    ]
    arriving = [
        pltpu.make_async_copy(source, target, sems.at[n])
        for n, (source, target) in enumerate(routes)
    ]
    for copy in arriving:
        copy.start()
    leaving = []

    def leave(source, target):
        leaving.append(pltpu.make_async_copy(source, target, out_sems.at[len(leaving)]))
        leaving[-1].start()

    def closed(n, piece, sums, slot, rows):
        terms = jnp.dot(metric[n, rows], piece[0, slot], preferred_element_type=jnp.float32)
        return (terms + sums[slot, rows]).astype(jnp.bfloat16)

    arriving[0].wait()
    for slot in range(2):
        arriving[2 + slot].wait()
        for rows in tiles(naux, 512):
            before[slot, rows] = closed(1, b2o, before_sum, slot, rows)
        leave(before.at[slot], before_out.at[slot])
    arriving[1].wait()
    column = jnp.broadcast_to(row[...], (128, nvir)).T[:, :1]
    pair_sum = column + row[...]
    total = jnp.zeros(density.shape, jnp.float32)
    for slot in range(2):
        arriving[4 + 2 * slot].wait()
        for rows in tiles(naux, 512):
            left[:, rows] = closed(0, b2s, own_sum, slot, rows).T
        for rnd, rights in enumerate((before, far)):
            if slot == 0 and rnd == 1:
                arriving[5].wait()
            local = ints[slot, rnd]
            meet = jnp.dot(left[...], rights[local], preferred_element_type=jnp.float32)
            gap = pair_sum - floats[0, slot] - floats[1 + rnd, local]
            kept = ints[slot, 2 + rnd].astype(jnp.float32)
            amp = (kept * meet / gap).astype(jnp.bfloat16)
            amps[slot, rnd] = amp
            total = total + lax.dot_general(
                amp, amp, (((1,), (1,)), ((), ())), preferred_element_type=jnp.float32
            )
        leave(amps.at[slot], amps_out.at[slot])
    density[...] = total.astype(jnp.bfloat16)
    leave(density, density_out)
    for copy in leaving:
        copy.wait()


def finish(ids, ints, floats, metric, own, before, far, b2s, b2o, row):
    _, naux, nvir = own.shape
    bf16 = jnp.bfloat16
    return pl.pallas_call(
        finish_kernel,
        out_shape=(
            jax.ShapeDtypeStruct((2, 2, nvir, nvir), bf16),
            jax.ShapeDtypeStruct((nvir, nvir), bf16),
            jax.ShapeDtypeStruct((2, naux, nvir), bf16),
        ),
        in_specs=[SMEM] * 3 + [HBM] * 4 + [VMEM] * 3,
        out_specs=(HBM, HBM, HBM),
        scratch_shapes=[
            pltpu.VMEM((2, naux, ROWS), bf16),
            pltpu.VMEM((2, naux, nvir), jnp.float32),
            pltpu.VMEM((2, naux, nvir), jnp.float32),
            pltpu.VMEM((2, naux, nvir), bf16),
            pltpu.VMEM((2, naux, nvir), bf16),
            pltpu.VMEM((2, 2, nvir, nvir), bf16),
            pltpu.VMEM((nvir, nvir), bf16),
            pltpu.VMEM((nvir, naux), bf16),
            pltpu.SemaphoreType.DMA((7,)),
            pltpu.SemaphoreType.DMA((5,)),
        ],
        compiler_params=params(58),
        cost_estimate=cost(
            8 * naux * ROWS * nvir + 8 * naux * nvir * nvir + 8 * nvir**3, 24 * naux * nvir
        ),
        name="finish",
    )(ids, ints, floats, metric, own, before, far, b2s, b2o, row)


def gradient_of(ints, amps, before, far, upper=None, tile=256):
    _, naux, nvir = before.shape
    steps = naux // tile // 2
    first = 0 if upper is None else steps
    rest = () if upper is None else (upper,)

    def kernel(ints, amps_hbm, before_hbm, far_hbm, *refs):
        out, amps, before, far, held, sems, out_sems = refs[-7:]
        ready = [pltpu.make_async_copy(amps_hbm, amps, sems.at[0])]
        for step in range(steps):
            there = slice((first + step) * tile, (first + step + 1) * tile)
            here = slice(step * tile, (step + 1) * tile)
            for n, (hbm, ref) in enumerate(((before_hbm, before), (far_hbm, far))):
                ready.append(
                    pltpu.make_async_copy(
                        hbm.at[:, there], ref.at[:, here], sems.at[1 + 2 * step + n]
                    )
                )
        for copy in ready:
            copy.start()
        ready[0].wait()
        copies = []
        for step in range(steps):
            there = slice((first + step) * tile, (first + step + 1) * tile)
            here = slice(step * tile, (step + 1) * tile)
            ready[1 + 2 * step].wait()
            ready[2 + 2 * step].wait()
            if step >= 2:
                copies[step - 2].wait()
            for slot in range(2):
                total = None
                for rnd, rights in enumerate((before, far)):
                    term = lax.dot_general(
                        rights[ints[slot, rnd], here],
                        amps[slot, rnd],
                        (((1,), (1,)), ((), ())),
                        preferred_element_type=jnp.float32,
                    )
                    total = term if total is None else total + term
                held[step % 2, :, slot, :] = total.astype(jnp.bfloat16)
            copies.append(
                pltpu.make_async_copy(held.at[step % 2], out.at[there], out_sems.at[step % 2])
            )
            copies[-1].start()
        for copy in copies[-2:]:
            copy.wait()

    bf16 = jnp.bfloat16
    return pl.pallas_call(
        kernel,
        out_shape=jax.ShapeDtypeStruct((naux, 2, nvir), bf16),
        in_specs=[SMEM, HBM, HBM, HBM] + [HBM] * len(rest),
        out_specs=HBM,
        scratch_shapes=[
            pltpu.VMEM((2, 2, nvir, nvir), bf16),
            pltpu.VMEM((2, naux // 2, nvir), bf16),
            pltpu.VMEM((2, naux // 2, nvir), bf16),
            pltpu.VMEM((2, tile, 2, nvir), bf16),
            pltpu.SemaphoreType.DMA((1 + 2 * steps,)),
            pltpu.SemaphoreType.DMA((2,)),
        ],
        input_output_aliases={4: 0} if rest else {},
        compiler_params=params(58),
        cost_estimate=cost(4 * naux * nvir * nvir, 6 * naux * nvir),
        name="gradient",
    )(ints, amps, before, far, *rest)


def summed_at_owner(array):
    pieces = array.reshape(16, -1, array.shape[1])
    arrived = lax.all_to_all(pieces, "occ", split_axis=0, concat_axis=0, tiled=True)
    return arrived.astype(jnp.float32).sum(axis=0)


def summed_for_everyone(array):
    copies = jnp.broadcast_to(array[None], (8, *array.shape))
    arrived = lax.all_to_all(copies, "aux", 0, 0, tiled=True)
    return arrived.astype(jnp.float32).sum(axis=0)


def on_device(integrals, metric, e_occ, e_vir, partner, screen):
    nvir = integrals.shape[-1]
    device = lax.axis_index(AXES)
    aux = lax.axis_index("aux")
    y, x_hi = aux // 2, aux % 2

    order = jnp.array([0, 1, 3, 2], jnp.int32)
    here = (y - order) % 4 * 2
    own_ids = jnp.concatenate([here + x_hi, here + 1 - x_hi]).astype(jnp.int32)
    shifted = (here + 6 * (1 - x_hi)) % 8
    before_ids = jnp.concatenate([shifted + x_hi, shifted + 1 - x_hi]).astype(jnp.int32)

    ints = jnp.concatenate([partner, screen], axis=1).astype(jnp.int32)
    owners = jnp.stack([device, (device - 1) % 128, (device - 64) % 128])
    floats = e_occ[owners[:, None] * 2 + jnp.arange(2)[None, :]]
    ids = jnp.stack([own_ids[7], before_ids[7]])
    even = x_hi == 0
    crosses = (device & 63) == 63
    row = e_vir[None, :]
    tables = (ints, floats, own_ids, before_ids, ids, row, even, crosses)

    by_owner = jnp.transpose(integrals, (1, 0, 2)).reshape(8, 2, ROWS, nvir)

    def block(index):
        return lax.dynamic_index_in_dim(by_owner, index, 0, True)

    def for_row(k):
        there = (y + k) % 4 * 2
        return block(there + x_hi), block(there + 1 - x_hi)

    even_only = lambda l: l & 1 == 0
    near0 = send(block((y * 2 + 7) % 8), to_row(0), (), even_only)
    y1 = send(jnp.concatenate(for_row(1)), along_y(1))
    y3 = send(jnp.concatenate(for_row(3)), along_y(3))
    near0, by_owner, same0, other0 = lax.optimization_barrier((near0, by_owner, *for_row(0)))
    a0s = send(same0, same_hop)
    a0o = send(other0, other_hop)
    third = jnp.concatenate(for_row(2))
    below0 = block((y * 2 + 5) % 8)
    y1, y3, a0s, a0o, near0, third, below0, tables = lax.optimization_barrier(
        (y1, y3, a0s, a0o, near0, third, below0, tables)
    )
    ints, floats, own_ids, before_ids, ids, row, even, crosses = tables

    same1 = jnp.concatenate([y1[:1], y3[:1]])
    a1s = send(same1, same_hop)
    a1o = send(jnp.concatenate([y1[1:], y3[1:]]), other_hop)
    half = send(third, along_y(3))
    r1 = send(jnp.concatenate([other0, y1[1:]]), next_row)
    own = transform(metric, own_ids, [(same0, 0, 0), (y1, 0, 1), (y3, 0, 2)])
    far = transform(metric, own_ids, [(a0s, 0, 0), (a0o, 0, 4)])
    passing0 = jnp.where(crosses, same0, a0s)
    a1s, a1o, half, r1, passing0, own, far = lax.optimization_barrier(
        (a1s, a1o, half, r1, passing0, own, far)
    )

    b0o = send(passing0, onward_hop)
    b1o = send(jnp.where(crosses, same1, a1s), onward_hop)
    b0s = send(a0o, same_hop)
    b1s = send(a1o, same_hop)
    y2 = send(half, along_y(3))
    far = transform(
        metric, own_ids, [(a1s, 0, 1), (a1s, 1, 2), (a1o, 0, 5), (a1o, 1, 6)], far
    )
    before = transform(metric, before_ids, [(r1, 0, 0), (r1, 1, 1)])
    y2, far, before = lax.optimization_barrier((y2, far, before))

    a2s = send(y2[:1], same_hop)
    a2o = send(y2[1:], other_hop)
    near3 = send(below0, to_row(3), (b1o,), even_only)
    own = transform(
        metric, own_ids, [(y2, 0, 3), (b0s, 0, 4), (b1s, 0, 5), (b1s, 1, 6)], own
    )
    before = transform(metric, before_ids, [(b0o, 0, 4), (b1o, 0, 5), (b1o, 1, 6)], before)
    a2s, a2o, y3, near0, near3, own, before = lax.optimization_barrier(
        (a2s, a2o, y3, near0, near3, own, before)
    )

    b2o = send(jnp.where(crosses, y2[:1], a2s), onward_hop)
    b2s = send(a2o, same_hop)
    near0 = jnp.where(even, near0, y3[1:])
    near3 = jnp.where(even, near3, y2[1:])
    far = transform(
        metric, own_ids, [(a2s, 0, 3), (a2o, 0, 7)], far, jnp.bfloat16
    )
    before = transform(
        metric, before_ids, [(near0, 0, 2), (near3, 0, 3)], before
    )

    amps, density, before = finish(ids, ints, floats, metric, own, before, far, b2s, b2o, row)
    rows = summed_at_owner(density).astype(jnp.bfloat16)
    gradient = gradient_of(ints, amps, before, far)
    rows, gradient = lax.optimization_barrier((rows, gradient))
    gradient = gradient_of(ints, amps, before, far, gradient)
    return gradient, summed_for_everyone(rows) / NOCC


def solution(mesh):
    placed = (P("aux", "occ", None), P(), P(), P(), P(AXES, None), P(AXES, None))
    return jax.shard_map(
        on_device,
        mesh=mesh,
        in_specs=placed,
        out_specs=(P(None, AXES, None), P("occ", None)),
        check_vma=False,
    )
```
